128 devices in a mesh: layer: 32 (over x, y, core), rows: 4 (over z).
Axes of the slice: x: 4, y: 4, z: 4, core: 2. Of those that a mesh axis runs over, the one named last changes fastest.
Arguments:
- weights: bfloat16 [256, 32, 288], P('layer'), may hold values from -0.375 to 0.375
- image: float32 [3, 32, 64, 128], P(None, None, 'rows'), may hold values from -6 to 6
- guess: float32 [64, 3, 32, 64, 128], P('layer', None, None, 'rows'), may hold values from -6 to 6
Outputs:
- corrected: float32 [64, 3, 32, 64, 128], P('layer', None, None, 'rows')
The draws below stay inside these ranges and needn't reach their ends.
All inputs are finite; a program needn't handle non-finite values.
Results may differ from the reference program's by a relative error of at most 0.009.
Values may be sent and summed in bfloat16 or wider, within the bound.
No kernel may reach another device: no remote copies, remote signals or barrier semaphores. Data moves between devices by JAX's collectives and lax.ppermute only.
A program may use at most 64 MiB of HBM per device.

```python
import jax
import jax.numpy as jnp
from jax import lax

C = 32
M = 4
L_DEV = 8
B = 3
IMG_W = 128
NL = 256
K = 64
IMG_ROWS = 64
N_LAYER = 32


def block_scale(own_key, shape, cuts, least, largest):
    loudness, own = 1.0, jax.random.fold_in(own_key, 6)
    for position, parts in cuts:
        steps = jnp.exp(jax.random.uniform(jax.random.fold_in(own, position), (parts,), jnp.float32, least / len(cuts), largest / len(cuts)))
        loudness = loudness * jnp.repeat(steps, shape[position] // parts).reshape([-1 if axis == position else 1 for axis in range(len(shape))])
    return loudness


def gaussian(rng, dims, spread, reach, split=(), held_as=jnp.bfloat16):
    array = jax.random.normal(rng, dims, jnp.float32) * spread
    if len(split) > 0:
        array = block_scale(rng, dims, split, -0.22, 0.18) * array
    return jnp.clip(array, min=-reach, max=reach).astype(held_as)


def setup_inputs(seed: int = 0) -> dict:
    keys = jax.random.split(jax.random.key(seed), 4)
    return {
        "weights": gaussian(keys[0], (NL, C, 9 * C), (9 * C) ** -0.5, 0.375, ((0, 32),)),
        "image": gaussian(keys[1], (B, C, IMG_ROWS, IMG_W), 1.0, 6.0, ((2, 4),), jnp.float32),
        "guess": gaussian(keys[2], (K, B, C, IMG_ROWS, IMG_W), 1.0, 6.0, ((0, 32), (3, 4)), jnp.float32),
    }


step_size = 0.125


def conv_layer(current, matrix):
    channels = current.shape[1]
    kernel = matrix.reshape(channels, 3, 3, channels).transpose(0, 3, 1, 2)
    return lax.conv_general_dilated(current.astype(jnp.bfloat16), kernel, (1, 1), ((1, 1), (1, 1)), dimension_numbers=("NCHW", "OIHW", "NCHW"), preferred_element_type=jnp.float32)


def reference(weights, image, guess):
    layers_all = L_DEV * N_LAYER
    points = layers_all // M
    stride = step_size
    grouped = weights.reshape(points, M, C, 9 * C)
    anchors = jnp.concatenate([image[None], guess[:-1]], axis=0)

    def interval(inputs):
        anchor, layer_w = inputs
        opening = conv_layer(anchor, layer_w[0])
        current = anchor + stride * jnp.tanh(opening)
        for j in range(1, M):
            current = current + stride * jnp.tanh(conv_layer(current, layer_w[j]))
        return current - (anchor + (M * stride) * jnp.tanh(opening))

    defects = lax.map(interval, (anchors, grouped))

    def advance(current, inputs):
        layer_w, defect = inputs
        updated = current + (M * stride) * jnp.tanh(conv_layer(current, layer_w)) + defect
        return updated, updated

    _, corrected = lax.scan(advance, image, (grouped[:, 0], defects))
    return corrected
```

```python
import functools

import jax
import jax.numpy as jnp
from jax import lax
from jax.experimental import pallas as pl
from jax.experimental.pallas import tpu as pltpu
from jax.sharding import PartitionSpec as P

M = 4
H = 0.125
C = 32
W = 128
BAND = 16
SUB = 8
STEPS = 2 * SUB
IMAGES = 3
WIN = 3 * BAND
REACH = 4
SPAN = BAND + 2 * REACH
PHASE = [BAND - 4 * q for q in range(4)]
OFFSET = [4 * sum(PHASE[:q]) for q in range(4)]
HALO = 4 * sum(PHASE)
CHUNK = 2 * BAND + 6
bf16 = jnp.bfloat16
f32 = jnp.float32


def home(b):
    return 2 * b


def taps(weights):
    n = weights.shape[0]
    w = weights.reshape(n, C, 3, 3, C).transpose(0, 3, 1, 2, 4).reshape(n, 3, C, 3 * C)
    return jnp.pad(w, ((0, 0), (0, 0), (0, 0), (0, W - 3 * C)))


def banded(tap):
    columns = []
    for dc in range(3):
        top = tap[dc]
        low = pltpu.roll(top.astype(f32), C, 1).astype(bf16)
        columns.append(jnp.concatenate([top, low], axis=0))
    return jnp.concatenate(columns, axis=1)


def spread(xs, buf, row, value):
    lane = lax.broadcasted_iota(jnp.int32, (2 * C, W), 1)
    left = jnp.where(lane == 0, 0.0, pltpu.roll(value, 1, 1))
    right = jnp.where(lane == W - 1, 0.0, pltpu.roll(value, W - 1, 1))
    for dc, v in enumerate((left, value, right)):
        xs[buf, dc, row : row + 2] = v.astype(bf16).reshape(2, C, W)


def block(xs, buf, matrix, row):
    parts = []
    for dc in range(3):
        a = xs[buf, dc, row : row + 4].reshape(4 * C, W)
        b = xs[buf, dc, row + 2 : row + 6].reshape(4 * C, W)
        parts.append(jnp.concatenate([a, b], axis=1))
    rhs = jnp.concatenate(parts, axis=0)
    z = jnp.dot(matrix, rhs, preferred_element_type=f32)
    return jnp.tanh(z[:, :W]), jnp.tanh(z[:, W:])


def clear_rims(xs, rows):
    for buf in range(2):
        for dc in range(3):
            for row in (0, rows + 1):
                xs[buf, dc, row] = jnp.zeros((C, W), bf16)


def relax_kernel(z_ref, own_ref, up_ref, dn_ref, img_ref, tap_ref, out_ref, v1_ref, xs, state, base):
    z = z_ref[0]
    clear_rims(xs, SPAN)
    low_ok = jnp.where(z > 0, 1.0, 0.0)
    high_ok = jnp.where(z < 3, 1.0, 0.0)

    def put(buf, pair, value):
        if pair < REACH // 2:
            value = value * low_ok
        elif pair >= (REACH + BAND) // 2:
            value = value * high_ok
        spread(xs, buf, 2 * pair + 1, value)

    def unit(u, carry):
        for pair in range(SPAN // 2):
            r = 2 * pair
            if r < REACH:
                x = up_ref[u, r : r + 2]
            elif r < REACH + BAND:
                x = own_ref[u, r - REACH : r - REACH + 2]
            else:
                x = dn_ref[u, r - REACH - BAND : r - REACH - BAND + 2]
            x = x.astype(f32).reshape(2 * C, W)
            state[r : r + 2] = x.reshape(2, C, W)
            put(0, pair, x)
        first = 4 * jnp.where(u == 2 * IMAGES, 2, u // IMAGES)
        for j in range(M):
            matrix = banded(tap_ref[first + j])
            for q in range(SPAN // 4):
                pair_t = block(xs, j % 2, matrix, 4 * q)
                for i, t in enumerate(pair_t):
                    r = 4 * q + 2 * i
                    x = state[r : r + 2].reshape(2 * C, W)
                    if j == 0 and REACH <= r < REACH + BAND:
                        base[r - REACH : r - REACH + 2] = (x + (M * H) * t).reshape(2, C, W)
                    x = x + H * t
                    state[r : r + 2] = x.reshape(2, C, W)
                    if j < M - 1:
                        put((j + 1) % 2, r // 2, x)

        @pl.when(u < 2 * IMAGES)
        def _():
            point, b = u // IMAGES, lax.rem(u, IMAGES)
            out_ref[b, pl.ds(point * BAND, BAND)] = (state[REACH : REACH + BAND] - base[...]).astype(bf16)

        @pl.when(u == 2 * IMAGES)
        def _():
            v1_ref[...] = img_ref[...] + (state[REACH : REACH + BAND] - own_ref[2 * IMAGES].astype(f32))

        return carry

    lax.fori_loop(0, 2 * IMAGES + 1, unit, 0)
    for b in range(IMAGES):
        out_ref[b, 2 * BAND : 2 * BAND + 3] = tap_ref[0]
        out_ref[b, 2 * BAND + 3 : 2 * BAND + 6] = tap_ref[4]


def pack_kernel(sub_ref, *refs):
    chunks, v1_ref, d_ref, w_ref, up_ref, dn_ref = refs[:SUB], refs[SUB], *refs[SUB + 1 :]
    sub = sub_ref[0]
    for r in range(SUB):
        at = lax.rem(sub + r, SUB)
        for p in range(2):
            d_ref[2 * at + p] = chunks[r][p * BAND : (p + 1) * BAND]
            w_ref[2 * at + p] = chunks[r][2 * BAND + 3 * p : 2 * BAND + 3 * p + 3]
    for q, rows in enumerate(PHASE):
        for s in range(4):
            to = OFFSET[q] + s * rows
            up_ref[to : to + rows] = d_ref[4 * q + s, BAND - rows :]
            dn_ref[to : to + rows] = d_ref[4 * q + s, :rows]
    v1 = v1_ref[...].astype(bf16)
    up_ref[HALO:] = v1
    dn_ref[HALO:] = v1


def sweep_kernel(
    info_ref, v1_ref, own_ref, above_ref, below_ref, d_ref, up_ref, dn_ref, w_ref,
    res_ref, out_ref, edge_ref, xs, state,
):
    z, sub, first = info_ref[0], info_ref[1], info_ref[2]
    clear_rims(xs, WIN)
    low_ok = jnp.where(z > 0, 1.0, 0.0)
    high_ok = jnp.where(z < 3, 1.0, 0.0)

    def put(buf, row, value):
        if row < BAND:
            value = value * low_ok
        elif row >= 2 * BAND:
            value = value * high_ok
        spread(xs, buf, row + 1, value)

    @pl.when(first == 1)
    def _():
        state[:BAND] = up_ref[HALO:].astype(f32)
        state[BAND : 2 * BAND] = v1_ref[...]
        state[2 * BAND :] = dn_ref[HALO:].astype(f32)

    @pl.when(first == 0)
    def _():
        state[:BAND] = above_ref[...].astype(f32)
        state[BAND : 2 * BAND] = own_ref[...]
        state[2 * BAND :] = below_ref[...].astype(f32)

    for row in range(0, WIN, 2):
        put(0, row, state[row : row + 2].reshape(2 * C, W))

    for q, rows in enumerate(PHASE):

        def step(i, carry, q=q, rows=rows):
            s = 4 * q + i
            now, later = lax.rem(s, 2), lax.rem(s + 1, 2)
            matrix = banded(w_ref[s])
            res_ref[lax.rem(s // 2 - sub + SUB, SUB), lax.rem(s, 2)] = xs[now, 1, BAND + 1 : 2 * BAND + 1]
            for row in range(BAND - rows, 2 * BAND + rows, 4):
                for k, t in enumerate(block(xs, now, matrix, row)):
                    r = row + 2 * k
                    if r < BAND:
                        at = OFFSET[q] + i * rows + (r - (BAND - rows))
                        d = up_ref[pl.ds(at, 2)]
                    elif r < 2 * BAND:
                        d = d_ref[s, r - BAND : r - BAND + 2]
                    else:
                        at = OFFSET[q] + i * rows + (r - 2 * BAND)
                        d = dn_ref[pl.ds(at, 2)]
                    x = state[r : r + 2].reshape(2 * C, W) + (M * H) * t + d.astype(f32).reshape(2 * C, W)
                    state[r : r + 2] = x.reshape(2, C, W)
                    put(later, r, x)
            return carry

        lax.fori_loop(0, 4, step, 0)
    out_ref[...] = state[BAND : 2 * BAND]
    edge_ref[...] = state[BAND : 2 * BAND].astype(bf16)


VM = pl.BlockSpec(memory_space=pltpu.VMEM)
SM = pl.BlockSpec(memory_space=pltpu.SMEM)


def shape(*dims, dtype=bf16):
    return jax.ShapeDtypeStruct(dims, dtype)


def relax(z, own, up, dn, image, tap):
    return pl.pallas_call(
        relax_kernel,
        out_shape=(shape(IMAGES, CHUNK, C, W), shape(BAND, C, W, dtype=f32)),
        in_specs=[SM] + [VM] * 5,
        out_specs=(VM, VM),
        scratch_shapes=[
            pltpu.VMEM((2, 3, SPAN + 2, C, W), bf16),
            pltpu.VMEM((SPAN, C, W), f32),
            pltpu.VMEM((BAND, C, W), f32),
        ],
        name="relax",
    )(z, own, up, dn, image, tap)


def pack(sub, chunks, v1):
    return pl.pallas_call(
        pack_kernel,
        out_shape=(
            shape(STEPS, BAND, C, W),
            shape(STEPS, 3, C, W),
            shape(HALO + BAND, C, W),
            shape(HALO + BAND, C, W),
        ),
        in_specs=[SM] + [VM] * (SUB + 1),
        out_specs=(VM,) * 4,
        name="pack",
    )(sub, *chunks, v1)


def sweep(info, *arrays):
    return pl.pallas_call(
        sweep_kernel,
        out_shape=(shape(SUB, 2, BAND, C, W), shape(BAND, C, W, dtype=f32), shape(BAND, C, W)),
        in_specs=[SM] + [VM] * 8,
        out_specs=(VM,) * 3,
        scratch_shapes=[
            pltpu.VMEM((2, 3, WIN + 2, C, W), bf16),
            pltpu.VMEM((WIN, C, W), f32),
        ],
        name="sweep",
    )(info, *arrays)


def per_device(weights, image, guess):
    layers, rows = lax.axis_size("layer"), lax.axis_size("rows")
    groups = layers // SUB
    l, z = lax.axis_index("layer"), lax.axis_index("rows")
    sub, group = lax.rem(l, SUB), l // SUB
    mine = jnp.minimum(sub // 2, IMAGES - 1)

    tap = taps(weights)
    following = lax.ppermute(tap[:M], "layer", [(i + 1, i) for i in range(layers - 1)])
    opening = tap[:M]
    for b in range(1, IMAGES):
        got = lax.ppermute(tap[:M], "layer", [(0, home(b))])
        opening = jnp.where(l == home(b), got, opening)
    tap = jnp.concatenate([tap[M:], following, opening], axis=0)

    own_image = lax.dynamic_index_in_dim(image, mine, 0, keepdims=False).transpose(1, 0, 2)
    points = guess.reshape(2 * IMAGES, C, BAND, W).transpose(0, 2, 1, 3).astype(bf16)
    points = jnp.concatenate([points, own_image.astype(bf16)[None]], axis=0)
    up = lax.ppermute(points[:, BAND - REACH :], "rows", [(i, i + 1) for i in range(rows - 1)])
    dn = lax.ppermute(points[:, :REACH], "rows", [(i + 1, i) for i in range(rows - 1)])

    zs = z.astype(jnp.int32).reshape(1)
    chunk, v1 = relax(zs, points, up, dn, own_image, tap)

    received = [lax.dynamic_index_in_dim(chunk, mine, 0, keepdims=False)]
    for r in range(1, SUB):
        target = jnp.clip(lax.rem(sub - r + SUB, SUB) // 2, 0, IMAGES - 1)
        value = lax.dynamic_index_in_dim(chunk, target, 0, keepdims=False)
        pairs = [
            (SUB * g + (home(b) + r) % SUB, SUB * g + home(b)) for g in range(groups) for b in range(IMAGES)
        ]
        received.append(lax.ppermute(value, "layer", pairs))
    d, w, up, dn = pack(sub.astype(jnp.int32).reshape(1), received, v1)
    above = lax.ppermute(up, "rows", [(i, i + 1) for i in range(rows - 1)])
    below = lax.ppermute(dn, "rows", [(i + 1, i) for i in range(rows - 1)])

    info = jnp.stack([z, sub, jnp.where(group == 0, 1, 0)]).astype(jnp.int32)
    def handoff(value, by):
        pairs = []
        for g in range(groups - 1):
            for b in range(IMAGES):
                for k in range(rows):
                    if 0 <= k + by < rows:
                        source = (SUB * g + home(b)) * rows + k
                        target = (SUB * (g + 1) + home(b)) * rows + k + by
                        pairs.append((source, target))
        return lax.ppermute(value, ("layer", "rows"), pairs)

    state, low, high = v1, above[HALO:], below[HALO:]
    for stage in range(groups):
        results, state, edge = sweep(info, v1, state, low, high, d, above, below, w)
        if stage < groups - 1:
            state, low, high = handoff(state, 0), handoff(edge, 1), handoff(edge, -1)

    slots = [results[0]]
    for r in range(1, SUB):
        pairs = [
            (SUB * g + home(b), SUB * g + (home(b) + r) % SUB) for g in range(groups) for b in range(IMAGES)
        ]
        slots.append(lax.ppermute(results[r], "layer", pairs))
    slots = jnp.stack(slots)
    images = [
        lax.dynamic_index_in_dim(slots, lax.rem(sub - home(b) + SUB, SUB), 0, keepdims=False)
        for b in range(IMAGES)
    ]
    return jnp.stack(images, axis=1).transpose(0, 1, 3, 2, 4).astype(f32)


def solution(mesh):
    return jax.shard_map(
        per_device,
        mesh=mesh,
        in_specs=(
            P("layer", None, None),
            P(None, None, "rows", None),
            P("layer", None, None, "rows", None),
        ),
        out_specs=P("layer", None, None, "rows", None),
        check_vma=False,
    )
```

```python
import functools

import jax
import jax.numpy as jnp
from jax import lax
from jax.experimental import pallas as pl
from jax.experimental.pallas import tpu as pltpu
from jax.sharding import PartitionSpec as P

M = 4
H = 0.125
C = 32
W = 128
BAND = 16
SUB = 8
STEPS = 2 * SUB
IMAGES = 3
WIN = 3 * BAND
REACH = 4
SPAN = BAND + 2 * REACH
PHASE = [BAND - 4 * q for q in range(4)]
OFFSET = [4 * sum(PHASE[:q]) for q in range(4)]
HALO = 4 * sum(PHASE)
CHUNK = 2 * BAND + 6
bf16 = jnp.bfloat16
f32 = jnp.float32


def home(b):
    return 2 * b


def taps(weights):
    n = weights.shape[0]
    w = weights.reshape(n, C, 3, 3, C).transpose(0, 3, 1, 2, 4).reshape(n, 3, C, 3 * C)
    return jnp.pad(w, ((0, 0), (0, 0), (0, 0), (0, W - 3 * C)))


def banded(tap):
    columns = []
    for dc in range(3):
        top = tap[dc]
        low = pltpu.roll(top.astype(f32), C, 1).astype(bf16)
        columns.append(jnp.concatenate([top, low], axis=0))
    return jnp.concatenate(columns, axis=1)


def spread(xs, buf, row, value):
    lane = lax.broadcasted_iota(jnp.int32, (2 * C, W), 1)
    left = jnp.where(lane == 0, 0.0, pltpu.roll(value, 1, 1))
    right = jnp.where(lane == W - 1, 0.0, pltpu.roll(value, W - 1, 1))
    for dc, v in enumerate((left, value, right)):
        xs[buf, dc, row : row + 2] = v.astype(bf16).reshape(2, C, W)


def block(xs, buf, matrix, row):
    parts = []
    for dc in range(3):
        a = xs[buf, dc, row : row + 4].reshape(4 * C, W)
        b = xs[buf, dc, row + 2 : row + 6].reshape(4 * C, W)
        parts.append(jnp.concatenate([a, b], axis=1))
    rhs = jnp.concatenate(parts, axis=0)
    z = jnp.dot(matrix, rhs, preferred_element_type=f32)
    return jnp.tanh(z[:, :W]), jnp.tanh(z[:, W:])


def clear_rims(xs, rows):
    for buf in range(2):
        for dc in range(3):
            for row in (0, rows + 1):
                xs[buf, dc, row] = jnp.zeros((C, W), bf16)


def relax_kernel(z_ref, own_ref, up_ref, dn_ref, img_ref, tap_ref, out_ref, v1_ref, xs, state, base):
    z = z_ref[0]
    clear_rims(xs, SPAN)
    low_ok = jnp.where(z > 0, 1.0, 0.0)
    high_ok = jnp.where(z < 3, 1.0, 0.0)

    def put(buf, pair, value):
        if pair < REACH // 2:
            value = value * low_ok
        elif pair >= (REACH + BAND) // 2:
            value = value * high_ok
        spread(xs, buf, 2 * pair + 1, value)

    def unit(u, carry):
        for pair in range(SPAN // 2):
            r = 2 * pair
            if r < REACH:
                x = up_ref[u, r : r + 2]
            elif r < REACH + BAND:
                x = own_ref[u, r - REACH : r - REACH + 2]
            else:
                x = dn_ref[u, r - REACH - BAND : r - REACH - BAND + 2]
            x = x.astype(f32).reshape(2 * C, W)
            state[r : r + 2] = x.reshape(2, C, W)
            put(0, pair, x)
        first = 4 * jnp.where(u == 2 * IMAGES, 2, u // IMAGES)
        for j in range(M):
            matrix = banded(tap_ref[first + j])
            for q in range(SPAN // 4):
                pair_t = block(xs, j % 2, matrix, 4 * q)
                for i, t in enumerate(pair_t):
                    r = 4 * q + 2 * i
                    x = state[r : r + 2].reshape(2 * C, W)
                    if j == 0 and REACH <= r < REACH + BAND:
                        base[r - REACH : r - REACH + 2] = (x + (M * H) * t).reshape(2, C, W)
                    x = x + H * t
                    state[r : r + 2] = x.reshape(2, C, W)
                    if j < M - 1:
                        put((j + 1) % 2, r // 2, x)

        @pl.when(u < 2 * IMAGES)
        def _():
            point, b = u // IMAGES, lax.rem(u, IMAGES)
            out_ref[b, pl.ds(point * BAND, BAND)] = (state[REACH : REACH + BAND] - base[...]).astype(bf16)

        @pl.when(u == 2 * IMAGES)
        def _():
            v1_ref[...] = img_ref[...] + (state[REACH : REACH + BAND] - own_ref[2 * IMAGES].astype(f32))

        return carry

    lax.fori_loop(0, 2 * IMAGES + 1, unit, 0)
    for b in range(IMAGES):
        out_ref[b, 2 * BAND : 2 * BAND + 3] = tap_ref[0]
        out_ref[b, 2 * BAND + 3 : 2 * BAND + 6] = tap_ref[4]


def pack_kernel(sub_ref, *refs):
    chunks, v1_ref, d_ref, w_ref, up_ref, dn_ref = refs[:SUB], refs[SUB], *refs[SUB + 1 :]
    sub = sub_ref[0]
    for r in range(SUB):
        at = lax.rem(sub + r, SUB)
        for p in range(2):
            d_ref[2 * at + p] = chunks[r][p * BAND : (p + 1) * BAND]
            w_ref[2 * at + p] = chunks[r][2 * BAND + 3 * p : 2 * BAND + 3 * p + 3]
    for q, rows in enumerate(PHASE):
        for s in range(4):
            to = OFFSET[q] + s * rows
            up_ref[to : to + rows] = d_ref[4 * q + s, BAND - rows :]
            dn_ref[to : to + rows] = d_ref[4 * q + s, :rows]
    v1 = v1_ref[...].astype(bf16)
    up_ref[HALO:] = v1
    dn_ref[HALO:] = v1


def sweep_kernel(
    info_ref, v1_ref, own_ref, above_ref, below_ref, d_ref, up_ref, dn_ref, w_ref,
    res_ref, out_ref, edge_ref, xs, state,
):
    z, sub, first = info_ref[0], info_ref[1], info_ref[2]
    clear_rims(xs, WIN)
    low_ok = jnp.where(z > 0, 1.0, 0.0)
    high_ok = jnp.where(z < 3, 1.0, 0.0)

    def put(buf, row, value):
        if row < BAND:
            value = value * low_ok
        elif row >= 2 * BAND:
            value = value * high_ok
        spread(xs, buf, row + 1, value)

    @pl.when(first == 1)
    def _():
        state[:BAND] = up_ref[HALO:].astype(f32)
        state[BAND : 2 * BAND] = v1_ref[...]
        state[2 * BAND :] = dn_ref[HALO:].astype(f32)

    @pl.when(first == 0)
    def _():
        state[:BAND] = above_ref[...].astype(f32)
        state[BAND : 2 * BAND] = own_ref[...]
        state[2 * BAND :] = below_ref[...].astype(f32)

    for row in range(0, WIN, 2):
        put(0, row, state[row : row + 2].reshape(2 * C, W))

    for q, rows in enumerate(PHASE):

        def two_steps(half, carry, q=q, rows=rows):
            for now in range(2):
                i = 2 * half + now
                s = 4 * q + i
                matrix = banded(w_ref[s])
                res_ref[lax.rem(2 * q + half - sub + SUB, SUB), now] = xs[now, 1, BAND + 1 : 2 * BAND + 1]
                for row in range(BAND - rows, 2 * BAND + rows, 4):
                    for k, t in enumerate(block(xs, now, matrix, row)):
                        r = row + 2 * k
                        if r < BAND:
                            at = OFFSET[q] + i * rows + (r - (BAND - rows))
                            d = up_ref[pl.ds(at, 2)]
                        elif r < 2 * BAND:
                            d = d_ref[s, r - BAND : r - BAND + 2]
                        else:
                            at = OFFSET[q] + i * rows + (r - 2 * BAND)
                            d = dn_ref[pl.ds(at, 2)]
                        x = state[r : r + 2].reshape(2 * C, W) + (M * H) * t + d.astype(f32).reshape(2 * C, W)
                        state[r : r + 2] = x.reshape(2, C, W)
                        put(1 - now, r, x)
            return carry

        lax.fori_loop(0, 2, two_steps, 0)
    out_ref[...] = state[BAND : 2 * BAND]
    edge_ref[...] = state[BAND : 2 * BAND].astype(bf16)


VM = pl.BlockSpec(memory_space=pltpu.VMEM)
SM = pl.BlockSpec(memory_space=pltpu.SMEM)


def shape(*dims, dtype=bf16):
    return jax.ShapeDtypeStruct(dims, dtype)


def relax(z, own, up, dn, image, tap):
    return pl.pallas_call(
        relax_kernel,
        out_shape=(shape(IMAGES, CHUNK, C, W), shape(BAND, C, W, dtype=f32)),
        in_specs=[SM] + [VM] * 5,
        out_specs=(VM, VM),
        scratch_shapes=[
            pltpu.VMEM((2, 3, SPAN + 2, C, W), bf16),
            pltpu.VMEM((SPAN, C, W), f32),
            pltpu.VMEM((BAND, C, W), f32),
        ],
        name="relax",
    )(z, own, up, dn, image, tap)


def pack(sub, chunks, v1):
    return pl.pallas_call(
        pack_kernel,
        out_shape=(
            shape(STEPS, BAND, C, W),
            shape(STEPS, 3, C, W),
            shape(HALO + BAND, C, W),
            shape(HALO + BAND, C, W),
        ),
        in_specs=[SM] + [VM] * (SUB + 1),
        out_specs=(VM,) * 4,
        name="pack",
    )(sub, *chunks, v1)


def sweep(info, *arrays):
    return pl.pallas_call(
        sweep_kernel,
        out_shape=(shape(SUB, 2, BAND, C, W), shape(BAND, C, W, dtype=f32), shape(BAND, C, W)),
        in_specs=[SM] + [VM] * 8,
        out_specs=(VM,) * 3,
        scratch_shapes=[
            pltpu.VMEM((2, 3, WIN + 2, C, W), bf16),
            pltpu.VMEM((WIN, C, W), f32),
        ],
        name="sweep",
    )(info, *arrays)


def per_device(weights, image, guess):
    layers, rows = lax.axis_size("layer"), lax.axis_size("rows")
    groups = layers // SUB
    l, z = lax.axis_index("layer"), lax.axis_index("rows")
    sub, group = lax.rem(l, SUB), l // SUB
    mine = jnp.minimum(sub // 2, IMAGES - 1)

    tap = taps(weights)
    following = lax.ppermute(tap[:M], "layer", [(i + 1, i) for i in range(layers - 1)])
    opening = tap[:M]
    for b in range(1, IMAGES):
        got = lax.ppermute(tap[:M], "layer", [(0, home(b))])
        opening = jnp.where(l == home(b), got, opening)
    tap = jnp.concatenate([tap[M:], following, opening], axis=0)

    own_image = lax.dynamic_index_in_dim(image, mine, 0, keepdims=False).transpose(1, 0, 2)
    points = guess.reshape(2 * IMAGES, C, BAND, W).transpose(0, 2, 1, 3).astype(bf16)
    points = jnp.concatenate([points, own_image.astype(bf16)[None]], axis=0)
    up = lax.ppermute(points[:, BAND - REACH :], "rows", [(i, i + 1) for i in range(rows - 1)])
    dn = lax.ppermute(points[:, :REACH], "rows", [(i + 1, i) for i in range(rows - 1)])

    zs = z.astype(jnp.int32).reshape(1)
    chunk, v1 = relax(zs, points, up, dn, own_image, tap)

    received = [lax.dynamic_index_in_dim(chunk, mine, 0, keepdims=False)]
    for r in range(1, SUB):
        target = jnp.clip(lax.rem(sub - r + SUB, SUB) // 2, 0, IMAGES - 1)
        value = lax.dynamic_index_in_dim(chunk, target, 0, keepdims=False)
        pairs = [
            (SUB * g + (home(b) + r) % SUB, SUB * g + home(b)) for g in range(groups) for b in range(IMAGES)
        ]
        received.append(lax.ppermute(value, "layer", pairs))
    d, w, up, dn = pack(sub.astype(jnp.int32).reshape(1), received, v1)

    def among_sweepers(value, ahead, by):
        pairs = []
        for g in range(groups - ahead):
            for b in range(IMAGES):
                for k in range(rows):
                    if 0 <= k + by < rows:
                        source = (SUB * g + home(b)) * rows + k
                        target = (SUB * (g + ahead) + home(b)) * rows + k + by
                        pairs.append((source, target))
        return lax.ppermute(value, ("layer", "rows"), pairs)

    above, below = among_sweepers(up, 0, 1), among_sweepers(dn, 0, -1)

    info = jnp.stack([z, sub, jnp.where(group == 0, 1, 0)]).astype(jnp.int32)
    state, low, high = v1, above[HALO:], below[HALO:]
    for stage in range(groups):
        results, state, edge = sweep(info, v1, state, low, high, d, above, below, w)
        if stage < groups - 1:
            state, low, high = among_sweepers(state, 1, 0), among_sweepers(edge, 1, 1), among_sweepers(edge, 1, -1)

    slots = [results[0]]
    for r in range(1, SUB):
        pairs = [
            (SUB * g + home(b), SUB * g + (home(b) + r) % SUB) for g in range(groups) for b in range(IMAGES)
        ]
        slots.append(lax.ppermute(results[r], "layer", pairs))
    slots = jnp.stack(slots)
    images = [
        lax.dynamic_index_in_dim(slots, lax.rem(sub - home(b) + SUB, SUB), 0, keepdims=False)
        for b in range(IMAGES)
    ]
    return jnp.stack(images, axis=1).transpose(0, 1, 3, 2, 4).astype(f32)


def solution(mesh):
    return jax.shard_map(
        per_device,
        mesh=mesh,
        in_specs=(
            P("layer", None, None),
            P(None, None, "rows", None),
            P("layer", None, None, "rows", None),
        ),
        out_specs=P("layer", None, None, "rows", None),
        check_vma=False,
    )
```

```python
import functools

import jax
import jax.numpy as jnp
from jax import lax
from jax.experimental import pallas as pl
from jax.experimental.pallas import tpu as pltpu
from jax.sharding import PartitionSpec as P

M = 4
H = 0.125
C = 32
W = 128
BAND = 16
SUB = 8
STEPS = 2 * SUB
IMAGES = 3
WIN = 3 * BAND
REACH = 4
SPAN = BAND + 2 * REACH
EDGE = [BAND - (s + 1) // 2 * 2 for s in range(STEPS)]
OFFSET = [sum(EDGE[:s]) for s in range(STEPS)]
HALO = sum(EDGE)
CHUNK = 2 * BAND + 6
bf16 = jnp.bfloat16
f32 = jnp.float32


FLOW = 4
HALVES = 2
LEAD = sum(EDGE[: STEPS // 2])


def home(b):
    return (0, 2, 6)[b]


def banded(tiles):
    lane = lax.broadcasted_iota(jnp.int32, (C, W), 1)
    keep = lane < 3 * C
    last, columns = jnp.zeros((C, W), bf16), []
    for tile in tiles:
        turned = pltpu.roll(tile, 3 * C, 1)
        columns.append(jnp.concatenate([tile, jnp.where(keep, last, turned)], axis=0))
        last = turned
    return jnp.concatenate(columns, axis=1)


def spread(xs, buf, row, value):
    lane = lax.broadcasted_iota(jnp.int32, (2 * C, W), 1)
    value = value.astype(bf16)
    left = jnp.where(lane == 0, bf16(0), pltpu.roll(value, 1, 1))
    right = jnp.where(lane == W - 1, bf16(0), pltpu.roll(value, W - 1, 1))
    for dc, v in enumerate((left, value, right)):
        xs[buf, row : row + 2, dc] = v.reshape(2, C, W)


def block(xs, buf, matrix, row):
    a = xs[buf, row : row + 4].reshape(12 * C, W)
    b = xs[buf, row + 2 : row + 6].reshape(12 * C, W)
    rhs = jnp.concatenate([a, b], axis=1)
    z = jnp.dot(matrix, rhs, preferred_element_type=f32)
    return jnp.tanh(z[:, :W]), jnp.tanh(z[:, W:])


def clear_rims(xs, rows):
    for buf in range(xs.shape[0]):
        for row in (0, rows + 1):
            xs[buf, row] = jnp.zeros((3, C, W), bf16)


def drain(source, targets, sems):
    copies = [pltpu.make_async_copy(source.at[r], target, sems.at[r]) for r, target in enumerate(targets)]
    for copy in copies:
        copy.start()
    for copy in copies:
        copy.wait()


def relax_kernel(info_ref, own_ref, up_ref, dn_ref, img_ref, here_ref, next_ref, open_ref, *refs):
    outs, (v1_ref, xs, state, base, slots, sems) = refs[:FLOW], refs[FLOW:]
    z, turn, lead = info_ref[0], info_ref[1], info_ref[2]

    def tiles(ref, n):
        tail = jnp.concatenate([ref[n, :, 2 * W :], jnp.zeros((C, 3 * C), bf16)], axis=1)
        return [ref[n, :, :W], ref[n, :, W : 2 * W], tail]

    def tap(point, j):
        return tiles(next_ref, j) if point else tiles(here_ref, M + j)

    clear_rims(xs, SPAN)
    low_ok = jnp.where(z > 0, 1.0, 0.0)
    high_ok = jnp.where(z < 3, 1.0, 0.0)

    def put(buf, pair, value):
        if pair < REACH // 2:
            value = value * low_ok
        elif pair >= (REACH + BAND) // 2:
            value = value * high_ok
        spread(xs, buf, 2 * pair + 1, value)

    def load(lane_set, u):
        for pair in range(SPAN // 2):
            r = 2 * pair
            if r < REACH:
                x = up_ref[u, r : r + 2]
            elif r >= REACH + BAND:
                x = dn_ref[u, r - REACH - BAND : r - REACH - BAND + 2]
            else:
                ref, at = (img_ref, 0) if isinstance(u, int) else (own_ref, u * (C * BAND))
                x = [ref[pl.ds(at + r - REACH + k, C, stride=BAND), :] for k in range(2)]
                x = jnp.concatenate(x, axis=0).astype(bf16)
            x = x.astype(f32).reshape(2 * C, W)
            state[lane_set, r : r + 2] = x.reshape(2, C, W)
            put(2 * lane_set, pair, x)

    def layer(lane_set, j, matrix):
        lo = (j + 1) // 2 * 2
        for row in range(lo, SPAN - lo, 4):
            for i, t in enumerate(block(xs, 2 * lane_set + j % 2, matrix, row)):
                r = row + 2 * i
                x = state[lane_set, r : r + 2].reshape(2 * C, W)
                if j == 0 and REACH <= r < REACH + BAND:
                    base[lane_set, r - REACH : r - REACH + 2] = (x + (M * H) * t).reshape(2, C, W)
                x = x + H * t
                state[lane_set, r : r + 2] = x.reshape(2, C, W)
                if j < M - 1:
                    put(2 * lane_set + (j + 1) % 2, r // 2, x)

    def image(b, carry):
        for point in range(2):
            load(point, point * IMAGES + b)
        for j in range(M):
            for point in range(2):
                layer(point, j, banded(tap(point, j)))
        slot = lax.rem(turn - b + FLOW, FLOW)
        for point in range(2):
            change = state[point, REACH : REACH + BAND] - base[point]
            slots[slot, point * BAND : (point + 1) * BAND] = change.astype(bf16)
            for t, tile in enumerate(tap(point, 0)):
                slots[slot, 2 * BAND + 3 * point + t] = tile
        return carry

    lax.fori_loop(0, IMAGES, image, 0)

    @pl.when(lead == 1)
    def _():
        load(0, 2 * IMAGES)
        for j in range(M):
            layer(0, j, banded(tiles(open_ref, j)))
        for r in range(BAND):
            x = img_ref[pl.ds(r, C, stride=BAND), :]
            v1_ref[r] = x + (state[0, REACH + r] - x.astype(bf16).astype(f32))

    drain(slots, outs, sems)


def rim_kernel(half, b_ref, *refs):
    chunks, rest = refs[:FLOW], refs[FLOW:]
    if half == 0:
        v1_ref, up_ref, dn_ref, d_ref = rest
        v1 = v1_ref[...].astype(bf16)
        up_ref[LEAD:] = v1
        dn_ref[LEAD:] = v1
    else:
        up_ref, dn_ref, d_ref = rest
    for k in range(FLOW):
        at = lax.rem(b_ref[0] + k, FLOW)
        for p in range(2):
            d_ref[2 * at + p] = chunks[k][p * BAND : (p + 1) * BAND]
    for s in range(SUB):
        rows, to = EDGE[SUB * half + s], OFFSET[SUB * half + s] - half * LEAD
        if rows:
            up_ref[to : to + rows] = d_ref[s, BAND - rows :]
            dn_ref[to : to + rows] = d_ref[s, :rows]


def order_kernel(b_ref, *refs):
    chunks, (d_ref, w_ref) = refs[:SUB], refs[SUB:]
    for r in range(SUB):
        at = SUB // 2 * (r // FLOW) + lax.rem(b_ref[0] + r % FLOW, FLOW)
        for p in range(2):
            d_ref[2 * at + p] = chunks[r][p * BAND : (p + 1) * BAND]
            w_ref[2 * at + p] = chunks[r][2 * BAND + 3 * p : 2 * BAND + 3 * p + 3]


def finish_kernel(info_ref, *refs):
    arrived, (out_ref, picked, stage, sems) = refs[:SUB], refs[SUB:]
    turn, half = info_ref[1], info_ref[4]
    for b in range(IMAGES):
        want = lax.rem(turn - b + FLOW, FLOW) + FLOW * half
        for r in range(SUB):

            @pl.when(want == r)
            def _():
                pltpu.make_async_copy(arrived[r], picked.at[b], sems.at[b]).start()

    for b in range(IMAGES):
        pltpu.make_async_copy(arrived[0], picked.at[b], sems.at[b]).wait()
        for p in range(2):
            stage[b, p] = picked[b, p].astype(f32).reshape(BAND * C, W)
            for c in range(C):
                to = ((p * IMAGES + b) * C + c) * BAND
                out_ref[to : to + BAND] = stage[b, p, pl.ds(c, BAND, stride=C), :]


def sweep_kernel(
    info_ref, v1_ref, own_ref, above_ref, below_ref, d_ref, up0_ref, dn0_ref, up1_ref, dn1_ref, w_ref,
    *refs,
):
    outs, (out_ref, edge_ref, xs, state, res_ref, sems) = refs[:SUB], refs[SUB:]
    z, first, b = info_ref[0], info_ref[2], info_ref[3]
    clear_rims(xs, WIN)
    low_ok = jnp.where(z > 0, 1.0, 0.0)
    high_ok = jnp.where(z < 3, 1.0, 0.0)

    def put(buf, row, value):
        if row < BAND:
            value = value * low_ok
        elif row >= 2 * BAND:
            value = value * high_ok
        spread(xs, buf, row + 1, value)

    @pl.when(first == 1)
    def _():
        state[:BAND] = up0_ref[LEAD:].astype(f32)
        state[BAND : 2 * BAND] = v1_ref[...]
        state[2 * BAND :] = dn0_ref[LEAD:].astype(f32)

    @pl.when(first == 0)
    def _():
        state[:BAND] = above_ref[...].astype(f32)
        state[BAND : 2 * BAND] = own_ref[...]
        state[2 * BAND :] = below_ref[...].astype(f32)

    for row in range(0, WIN, 2):
        put(0, row, state[row : row + 2].reshape(2 * C, W))

    for s, rows in enumerate(EDGE):
        now = s % 2
        matrix = banded([w_ref[s, t] for t in range(3)])
        half = s // SUB
        up_ref, dn_ref = (up1_ref, dn1_ref) if half else (up0_ref, dn0_ref)
        res_ref[FLOW * half + lax.rem(s // 2 % FLOW - b + FLOW, FLOW), now] = xs[now, BAND + 1 : 2 * BAND + 1, 1]
        for row in range(BAND - rows, 2 * BAND + rows, 4):
            for k, t in enumerate(block(xs, now, matrix, row)):
                r = row + 2 * k
                if r < BAND:
                    at = OFFSET[s] - half * LEAD + r - (BAND - rows)
                    d = up_ref[at : at + 2]
                elif r < 2 * BAND:
                    d = d_ref[s, r - BAND : r - BAND + 2]
                else:
                    at = OFFSET[s] - half * LEAD + r - 2 * BAND
                    d = dn_ref[at : at + 2]
                x = state[r : r + 2].reshape(2 * C, W) + ((M * H) * t + d.astype(f32).reshape(2 * C, W))
                state[r : r + 2] = x.reshape(2, C, W)
                if s < STEPS - 1:
                    put(1 - now, r, x)
    out_ref[...] = state[BAND : 2 * BAND]
    edge_ref[...] = state[BAND : 2 * BAND].astype(bf16)
    drain(res_ref, outs, sems)


VM = pl.BlockSpec(memory_space=pltpu.VMEM)
SM = pl.BlockSpec(memory_space=pltpu.SMEM)
AN = pl.BlockSpec(memory_space=pl.ANY)


def shape(*dims, dtype=bf16):
    return jax.ShapeDtypeStruct(dims, dtype)


def relax(info, *arrays):
    outs = pl.pallas_call(
        relax_kernel,
        out_shape=(shape(CHUNK, C, W),) * FLOW + (shape(BAND, C, W, dtype=f32),),
        in_specs=[SM] + [VM] * 7,
        out_specs=(AN,) * FLOW + (VM,),
        scratch_shapes=[
            pltpu.VMEM((4, SPAN + 2, 3, C, W), bf16),
            pltpu.VMEM((2, SPAN, C, W), f32),
            pltpu.VMEM((2, BAND, C, W), f32),
            pltpu.VMEM((FLOW, CHUNK, C, W), bf16),
            pltpu.SemaphoreType.DMA((FLOW,)),
        ],
        name="relax",
    )(info, *arrays)
    return outs[:FLOW], outs[FLOW]


def rims(half, b, *arrays):
    total = HALO - LEAD if half else LEAD + BAND
    return pl.pallas_call(
        functools.partial(rim_kernel, half),
        out_shape=(shape(total, C, W),) * 2,
        in_specs=[SM] + [VM] * len(arrays),
        out_specs=(VM, VM),
        scratch_shapes=[pltpu.VMEM((SUB, BAND, C, W), bf16)],
        name=f"rims{half}",
    )(b, *arrays)


def finish(info, arrays):
    return pl.pallas_call(
        finish_kernel,
        out_shape=shape(2 * IMAGES * C * BAND, W, dtype=f32),
        in_specs=[SM] + [AN] * SUB,
        out_specs=VM,
        scratch_shapes=[
            pltpu.VMEM((IMAGES, 2, BAND, C, W), bf16),
            pltpu.VMEM((IMAGES, 2, BAND * C, W), f32),
            pltpu.SemaphoreType.DMA((IMAGES,)),
        ],
        name="finish",
    )(info, *arrays)


def order(sub, chunks):
    return pl.pallas_call(
        order_kernel,
        out_shape=(shape(STEPS, BAND, C, W), shape(STEPS, 3, C, W)),
        in_specs=[SM] + [VM] * SUB,
        out_specs=(VM, VM),
        cost_estimate=pl.CostEstimate(flops=0, bytes_accessed=5_000_000, transcendentals=0),
        name="order",
    )(sub, *chunks)


def sweep(info, *arrays):
    outs = pl.pallas_call(
        sweep_kernel,
        out_shape=(shape(2, BAND, C, W),) * SUB + (shape(BAND, C, W, dtype=f32), shape(BAND, C, W)),
        in_specs=[SM] + [VM] * 10,
        out_specs=(AN,) * SUB + (VM, VM),
        scratch_shapes=[
            pltpu.VMEM((2, WIN + 2, 3, C, W), bf16),
            pltpu.VMEM((WIN, C, W), f32),
            pltpu.VMEM((SUB, 2, BAND, C, W), bf16),
            pltpu.SemaphoreType.DMA((SUB,)),
        ],
        name="sweep",
    )(info, *arrays)
    return outs[:SUB], outs[SUB], outs[SUB + 1]


def per_device(weights, image, guess):
    layers, rows = lax.axis_size("layer"), lax.axis_size("rows")
    groups = layers // SUB
    l, z = lax.axis_index("layer"), lax.axis_index("rows")
    sub, group = lax.rem(l, SUB), l // SUB
    mine = jnp.where(sub == home(1), 1, jnp.where(sub == home(2), 2, 0))

    own_image = lax.dynamic_index_in_dim(image, mine, 0, keepdims=False)
    flat = guess.reshape(2 * IMAGES, C, BAND, W)

    def edge_rows(first):
        rim = jnp.concatenate([flat[:, :, first : first + REACH], own_image[None, :, first : first + REACH]], axis=0)
        return rim.transpose(0, 2, 1, 3).astype(bf16)

    rim_up, rim_dn, small = lax.optimization_barrier((edge_rows(BAND - REACH), edge_rows(0), weights[:M]))
    up = lax.ppermute(rim_up, "rows", [(i, i + 1) for i in range(rows - 1)])
    dn = lax.ppermute(rim_dn, "rows", [(i + 1, i) for i in range(rows - 1)])
    following = lax.ppermute(small, "layer", [(i + 1, i) for i in range(layers - 1)])
    opening = small
    for b in range(1, IMAGES):
        got = lax.ppermute(small, "layer", [(0, home(b))])
        opening = jnp.where(l == home(b), got, opening)

    lead = jnp.where(group == 0, 1, 0)
    info = jnp.stack([z, lax.rem(sub, FLOW), lead, mine, sub // FLOW]).astype(jnp.int32)
    sends, v1 = relax(
        info, guess.reshape(-1, W), up, dn, own_image.reshape(-1, W), weights, following, opening
    )

    def pairs(half, k):
        return [
            (SUB * g + FLOW * half + (b + k) % FLOW, SUB * g + home(b))
            for g in range(groups)
            for b in range(IMAGES)
        ]

    received = [[lax.ppermute(sends[k], "layer", pairs(h, k)) for k in range(FLOW)] for h in range(HALVES)]

    def among_sweepers(value, ahead, by):
        pairs = []
        for g in range(groups - ahead):
            for b in range(IMAGES):
                for k in range(rows):
                    if 0 <= k + by < rows:
                        source = (SUB * g + home(b)) * rows + k
                        target = (SUB * (g + ahead) + home(b)) * rows + k + by
                        pairs.append((source, target))
        return lax.ppermute(value, ("layer", "rows"), pairs)

    images = mine.astype(jnp.int32).reshape(1)
    up, dn = rims(0, images, *received[0], v1)
    up0, dn0 = among_sweepers(up, 0, 1), among_sweepers(dn, 0, -1)
    up, dn = rims(1, images, *received[1])
    up1, dn1 = among_sweepers(up, 0, 1), among_sweepers(dn, 0, -1)
    d, w = order(images, received[0] + received[1])

    state = v1
    low = high = jnp.zeros((BAND, C, W), bf16)
    for stage in range(groups):
        results, state, edge = sweep(info, v1, state, low, high, d, up0, dn0, up1, dn1, w)
        if stage < groups - 1:
            state, low, high = among_sweepers(state, 1, 0), among_sweepers(edge, 1, 1), among_sweepers(edge, 1, -1)

    back = []
    for h in range(HALVES):
        for k in range(FLOW):
            back.append(lax.ppermute(results[FLOW * h + k], "layer", [(t, s) for s, t in pairs(h, k)]))
    return finish(info, back).reshape(guess.shape)


def solution(mesh):
    return jax.shard_map(
        per_device,
        mesh=mesh,
        in_specs=(
            P("layer", None, None),
            P(None, None, "rows", None),
            P("layer", None, None, "rows", None),
        ),
        out_specs=P("layer", None, None, "rows", None),
        check_vma=False,
    )
```

```python
import functools

import jax
import jax.numpy as jnp
from jax import lax
from jax.experimental import pallas as pl
from jax.experimental.pallas import tpu as pltpu
from jax.sharding import PartitionSpec as P


M = 4
H = 0.125
C = 32
W = 128
BAND = 16
SUB = 8
STEPS = 2 * SUB
IMAGES = 3
WIN = 3 * BAND
REACH = 4
SPAN = BAND + 2 * REACH
EDGE = [BAND - (s + 1) // 2 * 2 for s in range(STEPS)]
OFFSET = [sum(EDGE[:s]) for s in range(STEPS)]
HALO = sum(EDGE)
CHUNK = 2 * BAND + 6
bf16 = jnp.bfloat16
f32 = jnp.float32


FLOW = 4
HALVES = 2
LEAD = sum(EDGE[: STEPS // 2])


def home(b):
    return (0, 2, 6)[b]


def banded(tiles):
    lane = lax.broadcasted_iota(jnp.int32, (C, W), 1)
    keep = lane < 3 * C
    last, columns = jnp.zeros((C, W), bf16), []
    for tile in tiles:
        turned = pltpu.roll(tile, 3 * C, 1)
        columns.append(jnp.concatenate([tile, jnp.where(keep, last, turned)], axis=0))
        last = turned
    return jnp.concatenate(columns, axis=1)


def spread(xs, buf, row, value):
    lane = lax.broadcasted_iota(jnp.int32, (2 * C, W), 1)
    value = value.astype(bf16)
    left = jnp.where(lane == 0, bf16(0), pltpu.roll(value, 1, 1))
    right = jnp.where(lane == W - 1, bf16(0), pltpu.roll(value, W - 1, 1))
    for dc, v in enumerate((left, value, right)):
        xs[buf, row : row + 2, dc] = v.reshape(2, C, W)


def block(xs, buf, matrix, row):
    a = xs[buf, row : row + 4].reshape(12 * C, W)
    b = xs[buf, row + 2 : row + 6].reshape(12 * C, W)
    rhs = jnp.concatenate([a, b], axis=1)
    z = jnp.dot(matrix, rhs, preferred_element_type=f32)
    return jnp.tanh(z[:, :W]), jnp.tanh(z[:, W:])


def clear_rims(xs, rows):
    for buf in range(xs.shape[0]):
        for row in (0, rows + 1):
            xs[buf, row] = jnp.zeros((3, C, W), bf16)


def drain(source, targets, sems):
    copies = [pltpu.make_async_copy(source.at[r], target, sems.at[r]) for r, target in enumerate(targets)]
    for copy in copies:
        copy.start()
    for copy in copies:
        copy.wait()


def relax_kernel(info_ref, own_ref, up_ref, dn_ref, img_ref, here_ref, next_ref, open_ref, *refs):
    outs, (v1_ref, xs, state, base, slots, sems) = refs[:FLOW], refs[FLOW:]
    z, turn, lead = info_ref[0], info_ref[1], info_ref[2]

    def tiles(ref, n):
        tail = jnp.concatenate([ref[n, :, 2 * W :], jnp.zeros((C, 3 * C), bf16)], axis=1)
        return [ref[n, :, :W], ref[n, :, W : 2 * W], tail]

    def tap(point, j):
        return tiles(next_ref, j) if point else tiles(here_ref, M + j)

    clear_rims(xs, SPAN)
    low_ok = jnp.where(z > 0, 1.0, 0.0)
    high_ok = jnp.where(z < 3, 1.0, 0.0)

    def put(buf, pair, value):
        if pair < REACH // 2:
            value = value * low_ok
        elif pair >= (REACH + BAND) // 2:
            value = value * high_ok
        spread(xs, buf, 2 * pair + 1, value)

    def load(lane_set, u):
        for pair in range(SPAN // 2):
            r = 2 * pair
            if r < REACH:
                x = up_ref[u, r : r + 2]
            elif r >= REACH + BAND:
                x = dn_ref[u, r - REACH - BAND : r - REACH - BAND + 2]
            else:
                ref, at = (img_ref, 0) if isinstance(u, int) else (own_ref, u * (C * BAND))
                x = [ref[pl.ds(at + r - REACH + k, C, stride=BAND), :] for k in range(2)]
                x = jnp.concatenate(x, axis=0).astype(bf16)
            x = x.astype(f32).reshape(2 * C, W)
            state[lane_set, r : r + 2] = x.reshape(2, C, W)
            put(2 * lane_set, pair, x)

    def layer(lane_set, j, matrix):
        lo = (j + 1) // 2 * 2
        for row in range(lo, SPAN - lo, 4):
            for i, t in enumerate(block(xs, 2 * lane_set + j % 2, matrix, row)):
                r = row + 2 * i
                x = state[lane_set, r : r + 2].reshape(2 * C, W)
                if j == 0 and REACH <= r < REACH + BAND:
                    base[lane_set, r - REACH : r - REACH + 2] = (x + (M * H) * t).reshape(2, C, W)
                x = x + H * t
                state[lane_set, r : r + 2] = x.reshape(2, C, W)
                if j < M - 1:
                    put(2 * lane_set + (j + 1) % 2, r // 2, x)

    def image(b, carry):
        for point in range(2):
            load(point, point * IMAGES + b)
        for j in range(M):
            for point in range(2):
                layer(point, j, banded(tap(point, j)))
        slot = lax.rem(turn - b + FLOW, FLOW)
        for point in range(2):
            change = state[point, REACH : REACH + BAND] - base[point]
            slots[slot, point * BAND : (point + 1) * BAND] = change.astype(bf16)
            for t, tile in enumerate(tap(point, 0)):
                slots[slot, 2 * BAND + 3 * point + t] = tile
        return carry

    lax.fori_loop(0, IMAGES, image, 0)

    @pl.when(lead == 1)
    def _():
        load(0, 2 * IMAGES)
        for j in range(M):
            layer(0, j, banded(tiles(open_ref, j)))
        for r in range(BAND):
            x = img_ref[pl.ds(r, C, stride=BAND), :]
            v1_ref[r] = x + (state[0, REACH + r] - x.astype(bf16).astype(f32))

    drain(slots, outs, sems)


def rim_kernel(half, b_ref, *refs):
    chunks, rest = refs[:FLOW], refs[FLOW:]
    if half == 0:
        v1_ref, up_ref, dn_ref, d_ref = rest
        v1 = v1_ref[...].astype(bf16)
        up_ref[LEAD:] = v1
        dn_ref[LEAD:] = v1
    else:
        up_ref, dn_ref, d_ref = rest
    for k in range(FLOW):
        at = lax.rem(b_ref[0] + k, FLOW)
        for p in range(2):
            d_ref[2 * at + p] = chunks[k][p * BAND : (p + 1) * BAND]
    for s in range(SUB):
        rows, to = EDGE[SUB * half + s], OFFSET[SUB * half + s] - half * LEAD
        if rows:
            up_ref[to : to + rows] = d_ref[s, BAND - rows :]
            dn_ref[to : to + rows] = d_ref[s, :rows]


def order_kernel(b_ref, *refs):
    chunks, (d_ref, w_ref) = refs[:SUB], refs[SUB:]
    for r in range(SUB):
        at = SUB // 2 * (r // FLOW) + lax.rem(b_ref[0] + r % FLOW, FLOW)
        for p in range(2):
            d_ref[2 * at + p] = chunks[r][p * BAND : (p + 1) * BAND]
            w_ref[2 * at + p] = chunks[r][2 * BAND + 3 * p : 2 * BAND + 3 * p + 3]


def finish_kernel(info_ref, *refs):
    arrived, (out_ref, picked, stage, sems) = refs[:SUB], refs[SUB:]
    turn, half = info_ref[1], info_ref[4]
    for b in range(IMAGES):
        want = lax.rem(turn - b + FLOW, FLOW) + FLOW * half
        for r in range(SUB):

            @pl.when(want == r)
            def _():
                pltpu.make_async_copy(arrived[r], picked.at[b], sems.at[b]).start()

    for b in range(IMAGES):
        pltpu.make_async_copy(arrived[0], picked.at[b], sems.at[b]).wait()
        for p in range(2):
            stage[b, p] = picked[b, p].astype(f32).reshape(BAND * C, W)
            for c in range(C):
                to = ((p * IMAGES + b) * C + c) * BAND
                out_ref[to : to + BAND] = stage[b, p, pl.ds(c, BAND, stride=C), :]


def sweep_kernel(
    opening, closing, info_ref, v1_ref, d_ref, up0_ref, dn0_ref, up1_ref, dn1_ref, w_ref, *refs
):
    if not opening:
        (own_ref, above_ref, below_ref), refs = refs[:3], refs[3:]
    if closing:
        outs, (xs, state, res_ref, sems) = refs[:SUB], refs[SUB:]
    else:
        out_ref, edge_ref, xs, state = refs
    z, first, b = info_ref[0], info_ref[2], info_ref[3]
    clear_rims(xs, WIN)
    low_ok = jnp.where(z > 0, 1.0, 0.0)
    high_ok = jnp.where(z < 3, 1.0, 0.0)

    def put(buf, row, value):
        if row < BAND:
            value = value * low_ok
        elif row >= 2 * BAND:
            value = value * high_ok
        spread(xs, buf, row + 1, value)

    def begin():
        state[:BAND] = up0_ref[LEAD:].astype(f32)
        state[BAND : 2 * BAND] = v1_ref[...]
        state[2 * BAND :] = dn0_ref[LEAD:].astype(f32)

    def resume():
        state[:BAND] = above_ref[...].astype(f32)
        state[BAND : 2 * BAND] = own_ref[...]
        state[2 * BAND :] = below_ref[...].astype(f32)

    if opening:
        begin()
    else:
        pl.when(first == 1)(begin)
        pl.when(first == 0)(resume)

    for row in range(0, WIN, 2):
        put(0, row, state[row : row + 2].reshape(2 * C, W))

    for s, rows in enumerate(EDGE):
        now = s % 2
        half = s // SUB
        if closing:
            res_ref[FLOW * half + lax.rem(s // 2 % FLOW - b + FLOW, FLOW), now] = xs[now, BAND + 1 : 2 * BAND + 1, 1]
            if s == STEPS - 1:
                break
        matrix = banded([w_ref[s, t] for t in range(3)])
        up_ref, dn_ref = (up1_ref, dn1_ref) if half else (up0_ref, dn0_ref)
        for row in range(BAND - rows, 2 * BAND + rows, 4):
            for k, t in enumerate(block(xs, now, matrix, row)):
                r = row + 2 * k
                if r < BAND:
                    at = OFFSET[s] - half * LEAD + r - (BAND - rows)
                    d = up_ref[at : at + 2]
                elif r < 2 * BAND:
                    d = d_ref[s, r - BAND : r - BAND + 2]
                else:
                    at = OFFSET[s] - half * LEAD + r - 2 * BAND
                    d = dn_ref[at : at + 2]
                x = state[r : r + 2].reshape(2 * C, W) + ((M * H) * t + d.astype(f32).reshape(2 * C, W))
                state[r : r + 2] = x.reshape(2, C, W)
                if s < STEPS - 1:
                    put(1 - now, r, x)
    if closing:
        drain(res_ref, outs, sems)
    else:
        out_ref[...] = state[BAND : 2 * BAND]
        edge_ref[...] = state[BAND : 2 * BAND].astype(bf16)


VM = pl.BlockSpec(memory_space=pltpu.VMEM)
SM = pl.BlockSpec(memory_space=pltpu.SMEM)
AN = pl.BlockSpec(memory_space=pl.ANY)


def shape(*dims, dtype=bf16):
    return jax.ShapeDtypeStruct(dims, dtype)


def relax(info, *arrays):
    outs = pl.pallas_call(
        relax_kernel,
        out_shape=(shape(CHUNK, C, W),) * FLOW + (shape(BAND, C, W, dtype=f32),),
        in_specs=[SM] + [VM] * 7,
        out_specs=(AN,) * FLOW + (VM,),
        scratch_shapes=[
            pltpu.VMEM((4, SPAN + 2, 3, C, W), bf16),
            pltpu.VMEM((2, SPAN, C, W), f32),
            pltpu.VMEM((2, BAND, C, W), f32),
            pltpu.VMEM((FLOW, CHUNK, C, W), bf16),
            pltpu.SemaphoreType.DMA((FLOW,)),
        ],
        name="relax",
    )(info, *arrays)
    return outs[:FLOW], outs[FLOW]


def rims(half, b, *arrays):
    total = HALO - LEAD if half else LEAD + BAND
    return pl.pallas_call(
        functools.partial(rim_kernel, half),
        out_shape=(shape(total, C, W),) * 2,
        in_specs=[SM] + [VM] * len(arrays),
        out_specs=(VM, VM),
        scratch_shapes=[pltpu.VMEM((SUB, BAND, C, W), bf16)],
    )(b, *arrays)


def finish(info, arrays):
    return pl.pallas_call(
        finish_kernel,
        out_shape=shape(2 * IMAGES * C * BAND, W, dtype=f32),
        in_specs=[SM] + [AN] * SUB,
        out_specs=VM,
        scratch_shapes=[
            pltpu.VMEM((IMAGES, 2, BAND, C, W), bf16),
            pltpu.VMEM((IMAGES, 2, BAND * C, W), f32),
            pltpu.SemaphoreType.DMA((IMAGES,)),
        ],
        name="finish",
    )(info, *arrays)


def order(sub, chunks):
    return pl.pallas_call(
        order_kernel,
        out_shape=(shape(STEPS, BAND, C, W), shape(STEPS, 3, C, W)),
        in_specs=[SM] + [VM] * SUB,
        out_specs=(VM, VM),
        cost_estimate=pl.CostEstimate(flops=0, bytes_accessed=5_000_000, transcendentals=0),
        name="order",
    )(sub, *chunks)


def sweep(opening, closing, info, *arrays):
    if closing:
        out_shape = (shape(2, BAND, C, W),) * SUB
        extra = [pltpu.VMEM((SUB, 2, BAND, C, W), bf16), pltpu.SemaphoreType.DMA((SUB,))]
    else:
        out_shape = (shape(BAND, C, W, dtype=f32), shape(BAND, C, W))
        extra = []
    return pl.pallas_call(
        functools.partial(sweep_kernel, opening, closing),
        out_shape=out_shape,
        in_specs=[SM] + [VM] * len(arrays),
        out_specs=(AN,) * SUB if closing else (VM, VM),
        scratch_shapes=[pltpu.VMEM((2, WIN + 2, 3, C, W), bf16), pltpu.VMEM((WIN, C, W), f32)] + extra,
        name="sweep",
    )(info, *arrays)


def cycle(weights, image, guess):
    layers, rows = lax.axis_size("layer"), lax.axis_size("rows")
    groups = layers // SUB
    l, z = lax.axis_index("layer"), lax.axis_index("rows")
    sub, group = lax.rem(l, SUB), l // SUB
    mine = jnp.where(sub == home(1), 1, jnp.where(sub == home(2), 2, 0))

    own_image = lax.dynamic_index_in_dim(image, mine, 0, keepdims=False)
    flat = guess.reshape(2 * IMAGES, C, BAND, W)

    def edge_rows(first):
        rim = jnp.concatenate([flat[:, :, first : first + REACH], own_image[None, :, first : first + REACH]], axis=0)
        return rim.transpose(0, 2, 1, 3).astype(bf16)

    small = weights[:M]
    up = lax.ppermute(edge_rows(BAND - REACH), "rows", [(i, i + 1) for i in range(rows - 1)])
    dn = lax.ppermute(edge_rows(0), "rows", [(i + 1, i) for i in range(rows - 1)])
    following = lax.ppermute(small, "layer", [(i + 1, i) for i in range(layers - 1)])
    opening = small
    for b in range(1, IMAGES):
        got = lax.ppermute(small, "layer", [(0, home(b))])
        opening = jnp.where(l == home(b), got, opening)

    lead = jnp.where(group == 0, 1, 0)
    info = jnp.stack([z, lax.rem(sub, FLOW), lead, mine, sub // FLOW]).astype(jnp.int32)
    sends, v1 = relax(
        info, guess.reshape(-1, W), up, dn, own_image.reshape(-1, W), weights, following, opening
    )

    def pairs(half, k):
        return [
            (SUB * g + FLOW * half + (b + k) % FLOW, SUB * g + home(b))
            for g in range(groups)
            for b in range(IMAGES)
        ]

    received = [[lax.ppermute(sends[k], "layer", pairs(h, k)) for k in range(FLOW)] for h in range(HALVES)]

    def among_sweepers(value, ahead, by):
        pairs = []
        for g in range(groups - ahead):
            for b in range(IMAGES):
                for k in range(rows):
                    if 0 <= k + by < rows:
                        source = (SUB * g + home(b)) * rows + k
                        target = (SUB * (g + ahead) + home(b)) * rows + k + by
                        pairs.append((source, target))
        return lax.ppermute(value, ("layer", "rows"), pairs)

    images = mine.astype(jnp.int32).reshape(1)
    up, dn = rims(0, images, *received[0], v1)
    up0, dn0 = among_sweepers(up, 0, 1), among_sweepers(dn, 0, -1)
    up, dn = rims(1, images, *received[1])
    up1, dn1 = among_sweepers(up, 0, 1), among_sweepers(dn, 0, -1)
    d, w = order(images, received[0] + received[1])

    handed = ()
    for stage in range(groups - 1):
        state, edge = sweep(stage == 0, False, info, v1, d, up0, dn0, up1, dn1, w, *handed)
        handed = among_sweepers(state, 1, 0), among_sweepers(edge, 1, 1), among_sweepers(edge, 1, -1)
    results = sweep(False, True, info, v1, d, up0, dn0, up1, dn1, w, *handed)

    back = []
    for h in range(HALVES):
        for k in range(FLOW):
            back.append(lax.ppermute(results[FLOW * h + k], "layer", [(t, s) for s, t in pairs(h, k)]))
    return finish(info, back).reshape(guess.shape)


def solution(mesh):
    return jax.shard_map(
        cycle,
        mesh=mesh,
        in_specs=(
            P("layer", None, None),
            P(None, None, "rows", None),
            P("layer", None, None, "rows", None),
        ),
        out_specs=P("layer", None, None, "rows", None),
        check_vma=False,
    )
```

```python
import functools

import jax
import jax.numpy as jnp
from jax import lax
from jax.experimental import pallas as pl
from jax.experimental.pallas import tpu as pltpu
from jax.sharding import PartitionSpec as P


M = 4
H = 0.125
C = 32
W = 128
BAND = 16
SUB = 8
STEPS = 2 * SUB
IMAGES = 3
WIN = 3 * BAND
REACH = 4
SPAN = BAND + 2 * REACH
EDGE = [BAND - (s + 1) // 2 * 2 for s in range(STEPS)]
OFFSET = [sum(EDGE[:s]) for s in range(STEPS)]
HALO = sum(EDGE)
CHUNK = 2 * BAND + 6
bf16 = jnp.bfloat16
f32 = jnp.float32


FLOW = 4
HALVES = 2
LEAD = sum(EDGE[: STEPS // 2])


def home(b):
    return (0, 2, 6)[b]


def banded(tiles):
    lane = lax.broadcasted_iota(jnp.int32, (C, W), 1)
    keep = lane < 3 * C
    last, columns = jnp.zeros((C, W), bf16), []
    for tile in tiles:
        turned = pltpu.roll(tile, 3 * C, 1)
        columns.append(jnp.concatenate([tile, jnp.where(keep, last, turned)], axis=0))
        last = turned
    return jnp.concatenate(columns, axis=1)


def spread(xs, buf, row, value):
    lane = lax.broadcasted_iota(jnp.int32, (2 * C, W), 1)
    value = value.astype(bf16)
    left = jnp.where(lane == 0, bf16(0), pltpu.roll(value, 1, 1))
    right = jnp.where(lane == W - 1, bf16(0), pltpu.roll(value, W - 1, 1))
    for dc, v in enumerate((left, value, right)):
        xs[buf, row : row + 2, dc] = v.reshape(2, C, W)


def block(xs, buf, matrix, row):
    a = xs[buf, row : row + 4].reshape(12 * C, W)
    b = xs[buf, row + 2 : row + 6].reshape(12 * C, W)
    rhs = jnp.concatenate([a, b], axis=1)
    z = jnp.dot(matrix, rhs, preferred_element_type=f32)
    return jnp.tanh(z[:, :W]), jnp.tanh(z[:, W:])


def clear_rims(xs, rows):
    for buf in range(xs.shape[0]):
        for row in (0, rows + 1):
            xs[buf, row] = jnp.zeros((3, C, W), bf16)


def relaxer(info_ref, xs, state):
    low_ok = jnp.where(info_ref[0] > 0, 1.0, 0.0)
    high_ok = jnp.where(info_ref[0] < 3, 1.0, 0.0)

    def put(buf, row, value):
        if row < REACH:
            value = value * low_ok
        elif row >= REACH + BAND:
            value = value * high_ok
        spread(xs, buf, row + 1, value)

    def load(point, u, up_ref, own_ref, dn_ref, at):
        for r in range(0, SPAN, 2):
            if r < REACH:
                x = up_ref[u, r : r + 2]
            elif r >= REACH + BAND:
                x = dn_ref[u, r - REACH - BAND : r - REACH - BAND + 2]
            else:
                x = [own_ref[pl.ds(at + r - REACH + k, C, stride=BAND), :] for k in range(2)]
                x = jnp.concatenate(x, axis=0).astype(bf16)
            x = x.astype(f32).reshape(2 * C, W)
            state[point, r : r + 2] = x.reshape(2, C, W)
            put(2 * point, r, x)

    def layer(point, j, matrix, base=None):
        lo = (j + 1) // 2 * 2
        for row in range(lo, SPAN - lo, 4):
            for i, t in enumerate(block(xs, 2 * point + j % 2, matrix, row)):
                r = row + 2 * i
                x = state[point, r : r + 2].reshape(2 * C, W)
                if j == 0 and base is not None and REACH <= r < REACH + BAND:
                    base[point, r - REACH : r - REACH + 2] = (x + (M * H) * t).reshape(2, C, W)
                x = x + H * t
                state[point, r : r + 2] = x.reshape(2, C, W)
                if j < M - 1:
                    put(2 * point + (j + 1) % 2, r, x)

    return load, layer


def tiles(ref, n):
    tail = jnp.concatenate([ref[n, :, 2 * W :], jnp.zeros((C, 3 * C), bf16)], axis=1)
    return [ref[n, :, :W], ref[n, :, W : 2 * W], tail]


def drain(source, targets, sems):
    copies = [pltpu.make_async_copy(source.at[r], target, sems.at[r]) for r, target in enumerate(targets)]
    for copy in copies:
        copy.start()
    for copy in copies:
        copy.wait()


def relax_kernel(k, info_ref, own_ref, up_ref, dn_ref, here_ref, next_ref, out_ref, xs, state, base):
    b = lax.rem(info_ref[1] - k + FLOW, FLOW)
    load, layer = relaxer(info_ref, xs, state)

    def tap(point, j):
        return tiles(next_ref, j) if point else tiles(here_ref, M + j)

    @pl.when(b < IMAGES)
    def _():
        clear_rims(xs, SPAN)
        for point in range(2):
            u = point * IMAGES + b
            load(point, u, up_ref, own_ref, dn_ref, u * (C * BAND))
        for j in range(M):
            for point in range(2):
                layer(point, j, banded(tap(point, j)), base)
        for point in range(2):
            change = state[point, REACH : REACH + BAND] - base[point]
            out_ref[point * BAND : (point + 1) * BAND] = change.astype(bf16)
            for t, tile in enumerate(tap(point, 0)):
                out_ref[2 * BAND + 3 * point + t] = tile


def opening_kernel(info_ref, img_ref, up_ref, dn_ref, open_ref, v1_ref, xs, state):
    load, layer = relaxer(info_ref, xs, state)

    @pl.when(info_ref[2] == 1)
    def _():
        clear_rims(xs, SPAN)
        load(0, 2 * IMAGES, up_ref, img_ref, dn_ref, 0)
        for j in range(M):
            layer(0, j, banded(tiles(open_ref, j)))
        for r in range(BAND):
            x = img_ref[pl.ds(r, C, stride=BAND), :]
            v1_ref[r] = x + (state[0, REACH + r] - x.astype(bf16).astype(f32))


def rim_kernel(half, b_ref, *refs):
    chunks, rest = refs[:FLOW], refs[FLOW:]
    if half == 0:
        v1_ref, up_ref, dn_ref, d_ref = rest
        v1 = v1_ref[...].astype(bf16)
        up_ref[LEAD:] = v1
        dn_ref[LEAD:] = v1
    else:
        up_ref, dn_ref, d_ref = rest
    for k in range(FLOW):
        at = lax.rem(b_ref[0] + k, FLOW)
        for p in range(2):
            d_ref[2 * at + p] = chunks[k][p * BAND : (p + 1) * BAND]
    for s in range(SUB):
        rows, to = EDGE[SUB * half + s], OFFSET[SUB * half + s] - half * LEAD
        if rows:
            up_ref[to : to + rows] = d_ref[s, BAND - rows :]
            dn_ref[to : to + rows] = d_ref[s, :rows]


def order_kernel(b_ref, *refs):
    chunks, (d_ref, w_ref) = refs[:SUB], refs[SUB:]
    for r in range(SUB):
        at = SUB // 2 * (r // FLOW) + lax.rem(b_ref[0] + r % FLOW, FLOW)
        for p in range(2):
            d_ref[2 * at + p] = chunks[r][p * BAND : (p + 1) * BAND]
            w_ref[2 * at + p] = chunks[r][2 * BAND + 3 * p : 2 * BAND + 3 * p + 3]


def finish_kernel(info_ref, *refs):
    arrived, (out_ref, picked, stage, sems) = refs[:SUB], refs[SUB:]
    turn, half = info_ref[1], info_ref[4]
    for b in range(IMAGES):
        want = lax.rem(turn - b + FLOW, FLOW) + FLOW * half
        for r in range(SUB):

            @pl.when(want == r)
            def _():
                pltpu.make_async_copy(arrived[r], picked.at[b], sems.at[b]).start()

    for b in range(IMAGES):
        pltpu.make_async_copy(arrived[0], picked.at[b], sems.at[b]).wait()
        for p in range(2):
            stage[b, p] = picked[b, p].astype(f32).reshape(BAND * C, W)
            for c in range(C):
                to = ((p * IMAGES + b) * C + c) * BAND
                out_ref[to : to + BAND] = stage[b, p, pl.ds(c, BAND, stride=C), :]


def sweep_kernel(
    opening, closing, info_ref, v1_ref, d_ref, up0_ref, dn0_ref, up1_ref, dn1_ref, w_ref, *refs
):
    if not opening:
        (own_ref, above_ref, below_ref), refs = refs[:3], refs[3:]
    if closing:
        outs, (xs, state, res_ref, sems) = refs[:SUB], refs[SUB:]
    else:
        out_ref, edge_ref, xs, state = refs
    z, first, b = info_ref[0], info_ref[2], info_ref[3]
    clear_rims(xs, WIN)
    low_ok = jnp.where(z > 0, 1.0, 0.0)
    high_ok = jnp.where(z < 3, 1.0, 0.0)

    def put(buf, row, value):
        if row < BAND:
            value = value * low_ok
        elif row >= 2 * BAND:
            value = value * high_ok
        spread(xs, buf, row + 1, value)

    def begin():
        state[:BAND] = up0_ref[LEAD:].astype(f32)
        state[BAND : 2 * BAND] = v1_ref[...]
        state[2 * BAND :] = dn0_ref[LEAD:].astype(f32)

    def resume():
        state[:BAND] = above_ref[...].astype(f32)
        state[BAND : 2 * BAND] = own_ref[...]
        state[2 * BAND :] = below_ref[...].astype(f32)

    if opening:
        begin()
    else:
        pl.when(first == 1)(begin)
        pl.when(first == 0)(resume)

    for row in range(0, WIN, 2):
        put(0, row, state[row : row + 2].reshape(2 * C, W))

    for s, rows in enumerate(EDGE):
        now = s % 2
        half = s // SUB
        if closing:
            res_ref[FLOW * half + lax.rem(s // 2 % FLOW - b + FLOW, FLOW), now] = xs[now, BAND + 1 : 2 * BAND + 1, 1]
            if s == STEPS - 1:
                break
        matrix = banded([w_ref[s, t] for t in range(3)])
        up_ref, dn_ref = (up1_ref, dn1_ref) if half else (up0_ref, dn0_ref)
        for row in range(BAND - rows, 2 * BAND + rows, 4):
            for k, t in enumerate(block(xs, now, matrix, row)):
                r = row + 2 * k
                if r < BAND:
                    at = OFFSET[s] - half * LEAD + r - (BAND - rows)
                    d = up_ref[at : at + 2]
                elif r < 2 * BAND:
                    d = d_ref[s, r - BAND : r - BAND + 2]
                else:
                    at = OFFSET[s] - half * LEAD + r - 2 * BAND
                    d = dn_ref[at : at + 2]
                x = state[r : r + 2].reshape(2 * C, W) + ((M * H) * t + d.astype(f32).reshape(2 * C, W))
                state[r : r + 2] = x.reshape(2, C, W)
                if s < STEPS - 1:
                    put(1 - now, r, x)
    if closing:
        drain(res_ref, outs, sems)
    else:
        out_ref[...] = state[BAND : 2 * BAND]
        edge_ref[...] = state[BAND : 2 * BAND].astype(bf16)


VM = pl.BlockSpec(memory_space=pltpu.VMEM)
SM = pl.BlockSpec(memory_space=pltpu.SMEM)
AN = pl.BlockSpec(memory_space=pl.ANY)


def shape(*dims, dtype=bf16):
    return jax.ShapeDtypeStruct(dims, dtype)


def relax(k, info, *arrays):
    return pl.pallas_call(
        functools.partial(relax_kernel, k),
        out_shape=shape(CHUNK, C, W),
        in_specs=[SM] + [VM] * len(arrays),
        out_specs=VM,
        scratch_shapes=[
            pltpu.VMEM((4, SPAN + 2, 3, C, W), bf16),
            pltpu.VMEM((2, SPAN, C, W), f32),
            pltpu.VMEM((2, BAND, C, W), f32),
        ],
    )(info, *arrays)


def opened(info, *arrays):
    return pl.pallas_call(
        opening_kernel,
        out_shape=shape(BAND, C, W, dtype=f32),
        in_specs=[SM] + [VM] * len(arrays),
        out_specs=VM,
        scratch_shapes=[
            pltpu.VMEM((2, SPAN + 2, 3, C, W), bf16),
            pltpu.VMEM((1, SPAN, C, W), f32),
        ],
        name="opening",
    )(info, *arrays)


def rims(half, b, *arrays):
    total = HALO - LEAD if half else LEAD + BAND
    return pl.pallas_call(
        functools.partial(rim_kernel, half),
        out_shape=(shape(total, C, W),) * 2,
        in_specs=[SM] + [VM] * len(arrays),
        out_specs=(VM, VM),
        scratch_shapes=[pltpu.VMEM((SUB, BAND, C, W), bf16)],
    )(b, *arrays)


def finish(info, arrays):
    return pl.pallas_call(
        finish_kernel,
        out_shape=shape(2 * IMAGES * C * BAND, W, dtype=f32),
        in_specs=[SM] + [AN] * SUB,
        out_specs=VM,
        scratch_shapes=[
            pltpu.VMEM((IMAGES, 2, BAND, C, W), bf16),
            pltpu.VMEM((IMAGES, 2, BAND * C, W), f32),
            pltpu.SemaphoreType.DMA((IMAGES,)),
        ],
        name="finish",
    )(info, *arrays)


def order(sub, chunks):
    return pl.pallas_call(
        order_kernel,
        out_shape=(shape(STEPS, BAND, C, W), shape(STEPS, 3, C, W)),
        in_specs=[SM] + [VM] * SUB,
        out_specs=(VM, VM),
        cost_estimate=pl.CostEstimate(flops=0, bytes_accessed=5_000_000, transcendentals=0),
        name="order",
    )(sub, *chunks)


def sweep(opening, closing, info, *arrays):
    if closing:
        out_shape = (shape(2, BAND, C, W),) * SUB
        extra = [pltpu.VMEM((SUB, 2, BAND, C, W), bf16), pltpu.SemaphoreType.DMA((SUB,))]
    else:
        out_shape = (shape(BAND, C, W, dtype=f32), shape(BAND, C, W))
        extra = []
    return pl.pallas_call(
        functools.partial(sweep_kernel, opening, closing),
        out_shape=out_shape,
        in_specs=[SM] + [VM] * len(arrays),
        out_specs=(AN,) * SUB if closing else (VM, VM),
        scratch_shapes=[pltpu.VMEM((2, WIN + 2, 3, C, W), bf16), pltpu.VMEM((WIN, C, W), f32)] + extra,
        name="sweep",
    )(info, *arrays)


def cycle(weights, image, guess):
    layers, rows = lax.axis_size("layer"), lax.axis_size("rows")
    groups = layers // SUB
    l, z = lax.axis_index("layer"), lax.axis_index("rows")
    sub, group = lax.rem(l, SUB), l // SUB
    mine = jnp.where(sub == home(1), 1, jnp.where(sub == home(2), 2, 0))

    own_image = lax.dynamic_index_in_dim(image, mine, 0, keepdims=False)
    flat = guess.reshape(2 * IMAGES, C, BAND, W)

    def edge_rows(first):
        rim = jnp.concatenate([flat[:, :, first : first + REACH], own_image[None, :, first : first + REACH]], axis=0)
        return rim.transpose(0, 2, 1, 3).astype(bf16)

    small = weights[:M]
    up = lax.ppermute(edge_rows(BAND - REACH), "rows", [(i, i + 1) for i in range(rows - 1)])
    dn = lax.ppermute(edge_rows(0), "rows", [(i + 1, i) for i in range(rows - 1)])
    following = lax.ppermute(small, "layer", [(i + 1, i) for i in range(layers - 1)])
    opening = small
    for b in range(1, IMAGES):
        got = lax.ppermute(small, "layer", [(0, home(b))])
        opening = jnp.where(l == home(b), got, opening)

    lead = jnp.where(group == 0, 1, 0)
    info = jnp.stack([z, lax.rem(sub, FLOW), lead, mine, sub // FLOW]).astype(jnp.int32)

    def pairs(half, k):
        return [
            (SUB * g + FLOW * half + (b + k) % FLOW, SUB * g + home(b))
            for g in range(groups)
            for b in range(IMAGES)
        ]

    received = [[], []]
    for k in range(FLOW):
        chunk = relax(k, info, guess.reshape(-1, W), up, dn, weights, following)
        for h in range(HALVES):
            received[h].append(lax.ppermute(chunk, "layer", pairs(h, k)))
    v1 = opened(info, own_image.reshape(-1, W), up, dn, opening)

    def among_sweepers(value, ahead, by):
        pairs = []
        for g in range(groups - ahead):
            for b in range(IMAGES):
                for k in range(rows):
                    if 0 <= k + by < rows:
                        source = (SUB * g + home(b)) * rows + k
                        target = (SUB * (g + ahead) + home(b)) * rows + k + by
                        pairs.append((source, target))
        return lax.ppermute(value, ("layer", "rows"), pairs)

    images = mine.astype(jnp.int32).reshape(1)
    up, dn = rims(0, images, *received[0], v1)
    up0, dn0 = among_sweepers(up, 0, 1), among_sweepers(dn, 0, -1)
    up, dn = rims(1, images, *received[1])
    up1, dn1 = among_sweepers(up, 0, 1), among_sweepers(dn, 0, -1)
    d, w = order(images, received[0] + received[1])

    handed = ()
    for stage in range(groups - 1):
        state, edge = sweep(stage == 0, False, info, v1, d, up0, dn0, up1, dn1, w, *handed)
        handed = among_sweepers(state, 1, 0), among_sweepers(edge, 1, 1), among_sweepers(edge, 1, -1)
    results = sweep(False, True, info, v1, d, up0, dn0, up1, dn1, w, *handed)

    back = []
    for h in range(HALVES):
        for k in range(FLOW):
            back.append(lax.ppermute(results[FLOW * h + k], "layer", [(t, s) for s, t in pairs(h, k)]))
    return finish(info, back).reshape(guess.shape)


def solution(mesh):
    return jax.shard_map(
        cycle,
        mesh=mesh,
        in_specs=(
            P("layer", None, None),
            P(None, None, "rows", None),
            P("layer", None, None, "rows", None),
        ),
        out_specs=P("layer", None, None, "rows", None),
        check_vma=False,
    )
```

```python
import functools

import jax
import jax.numpy as jnp
from jax import lax
from jax.experimental import pallas as pl
from jax.experimental.pallas import tpu as pltpu
from jax.sharding import PartitionSpec as P


M = 4
H = 0.125
C = 32
W = 128
BAND = 16
SUB = 8
STEPS = 2 * SUB
IMAGES = 3
WIN = 3 * BAND
REACH = 4
SPAN = BAND + 2 * REACH
EDGE = [BAND - (s + 1) // 2 * 2 for s in range(STEPS)]
OFFSET = [sum(EDGE[:s]) for s in range(STEPS)]
HALO = sum(EDGE)
CHUNK = 2 * BAND + 6
bf16 = jnp.bfloat16
f32 = jnp.float32


FLOW = 4
HALVES = 2
LEAD = sum(EDGE[: STEPS // 2])


def home(b):
    return (0, 2, 6)[b]


def banded(tiles):
    lane = lax.broadcasted_iota(jnp.int32, (C, W), 1)
    keep = lane < 3 * C
    last, columns = jnp.zeros((C, W), bf16), []
    for tile in tiles:
        turned = pltpu.roll(tile, 3 * C, 1)
        columns.append(jnp.concatenate([tile, jnp.where(keep, last, turned)], axis=0))
        last = turned
    return jnp.concatenate(columns, axis=1)


def spread(xs, buf, row, value):
    lane = lax.broadcasted_iota(jnp.int32, (2 * C, W), 1)
    value = value.astype(bf16)
    left = jnp.where(lane == 0, bf16(0), pltpu.roll(value, 1, 1))
    right = jnp.where(lane == W - 1, bf16(0), pltpu.roll(value, W - 1, 1))
    for dc, v in enumerate((left, value, right)):
        xs[buf, row : row + 2, dc] = v.reshape(2, C, W)


def block(xs, buf, matrix, row):
    a = xs[buf, row : row + 4].reshape(12 * C, W)
    b = xs[buf, row + 2 : row + 6].reshape(12 * C, W)
    rhs = jnp.concatenate([a, b], axis=1)
    z = jnp.dot(matrix, rhs, preferred_element_type=f32)
    return jnp.tanh(z[:, :W]), jnp.tanh(z[:, W:])


def clear_rims(xs, rows):
    for buf in range(xs.shape[0]):
        for row in (0, rows + 1):
            xs[buf, row] = jnp.zeros((3, C, W), bf16)


def drain(source, targets, sems):
    copies = [pltpu.make_async_copy(source.at[r], target, sems.at[r]) for r, target in enumerate(targets)]
    for copy in copies:
        copy.start()
    for copy in copies:
        copy.wait()


def relax_kernel(info_ref, own_ref, up_ref, dn_ref, img_ref, here_ref, next_ref, open_ref, *refs):
    outs, (v1_ref, xs, state, base, slots, sems) = refs[:FLOW], refs[FLOW:]
    z, turn, lead = info_ref[0], info_ref[1], info_ref[2]

    def tiles(ref, n):
        tail = jnp.concatenate([ref[n, :, 2 * W :], jnp.zeros((C, 3 * C), bf16)], axis=1)
        return [ref[n, :, :W], ref[n, :, W : 2 * W], tail]

    def tap(point, j):
        return tiles(next_ref, j) if point else tiles(here_ref, M + j)

    clear_rims(xs, SPAN)
    low_ok = jnp.where(z > 0, 1.0, 0.0)
    high_ok = jnp.where(z < 3, 1.0, 0.0)

    def put(buf, pair, value):
        if pair < REACH // 2:
            value = value * low_ok
        elif pair >= (REACH + BAND) // 2:
            value = value * high_ok
        spread(xs, buf, 2 * pair + 1, value)

    def load(lane_set, u):
        for pair in range(SPAN // 2):
            r = 2 * pair
            if r < REACH:
                x = up_ref[u, r : r + 2]
            elif r >= REACH + BAND:
                x = dn_ref[u, r - REACH - BAND : r - REACH - BAND + 2]
            else:
                ref, at = (img_ref, 0) if isinstance(u, int) else (own_ref, u * (C * BAND))
                x = [ref[pl.ds(at + r - REACH + k, C, stride=BAND), :] for k in range(2)]
                x = jnp.concatenate(x, axis=0).astype(bf16)
            x = x.astype(f32).reshape(2 * C, W)
            state[lane_set, r : r + 2] = x.reshape(2, C, W)
            put(2 * lane_set, pair, x)

    def layer(lane_set, j, matrix):
        lo = (j + 1) // 2 * 2
        for row in range(lo, SPAN - lo, 4):
            for i, t in enumerate(block(xs, 2 * lane_set + j % 2, matrix, row)):
                r = row + 2 * i
                x = state[lane_set, r : r + 2].reshape(2 * C, W)
                if j == 0 and REACH <= r < REACH + BAND:
                    base[lane_set, r - REACH : r - REACH + 2] = (x + (M * H) * t).reshape(2, C, W)
                x = x + H * t
                state[lane_set, r : r + 2] = x.reshape(2, C, W)
                if j < M - 1:
                    put(2 * lane_set + (j + 1) % 2, r // 2, x)

    def image(b, carry):
        for point in range(2):
            load(point, point * IMAGES + b)
        for j in range(M):
            for point in range(2):
                layer(point, j, banded(tap(point, j)))
        slot = lax.rem(turn - b + FLOW, FLOW)
        for point in range(2):
            change = state[point, REACH : REACH + BAND] - base[point]
            slots[slot, point * BAND : (point + 1) * BAND] = change.astype(bf16)
            for t, tile in enumerate(tap(point, 0)):
                slots[slot, 2 * BAND + 3 * point + t] = tile
        return carry

    lax.fori_loop(0, IMAGES, image, 0)

    @pl.when(lead == 1)
    def _():
        load(0, 2 * IMAGES)
        for j in range(M):
            layer(0, j, banded(tiles(open_ref, j)))
        for r in range(BAND):
            x = img_ref[pl.ds(r, C, stride=BAND), :]
            v1_ref[r] = x + (state[0, REACH + r] - x.astype(bf16).astype(f32))

    drain(slots, outs, sems)


def rim_kernel(half, b_ref, *refs):
    chunks, rest = refs[:FLOW], refs[FLOW:]
    if half == 0:
        v1_ref, up_ref, dn_ref, d_ref = rest
        v1 = v1_ref[...].astype(bf16)
        up_ref[LEAD:] = v1
        dn_ref[LEAD:] = v1
    else:
        up_ref, dn_ref, d_ref = rest
    for k in range(FLOW):
        at = lax.rem(b_ref[0] + k, FLOW)
        for p in range(2):
            d_ref[2 * at + p] = chunks[k][p * BAND : (p + 1) * BAND]
    for s in range(SUB):
        rows, to = EDGE[SUB * half + s], OFFSET[SUB * half + s] - half * LEAD
        if rows:
            up_ref[to : to + rows] = d_ref[s, BAND - rows :]
            dn_ref[to : to + rows] = d_ref[s, :rows]


def order_kernel(b_ref, *refs):
    chunks, (d_ref, w_ref) = refs[:SUB], refs[SUB:]
    for r in range(SUB):
        at = SUB // 2 * (r // FLOW) + lax.rem(b_ref[0] + r % FLOW, FLOW)
        for p in range(2):
            d_ref[2 * at + p] = chunks[r][p * BAND : (p + 1) * BAND]
            w_ref[2 * at + p] = chunks[r][2 * BAND + 3 * p : 2 * BAND + 3 * p + 3]


def finish_kernel(info_ref, *refs):
    arrived, (out_ref, picked, stage, sems) = refs[:SUB], refs[SUB:]
    turn, half = info_ref[1], info_ref[4]
    for b in range(IMAGES):
        want = lax.rem(turn - b + FLOW, FLOW) + FLOW * half
        for r in range(SUB):

            @pl.when(want == r)
            def _():
                pltpu.make_async_copy(arrived[r], picked.at[b], sems.at[b]).start()

    for b in range(IMAGES):
        pltpu.make_async_copy(arrived[0], picked.at[b], sems.at[b]).wait()
        for p in range(2):
            stage[b, p] = picked[b, p].astype(f32).reshape(BAND * C, W)
            for c in range(C):
                to = ((p * IMAGES + b) * C + c) * BAND
                out_ref[to : to + BAND] = stage[b, p, pl.ds(c, BAND, stride=C), :]


def sweep_kernel(
    opening, closing, info_ref, v1_ref, d_ref, up0_ref, dn0_ref, up1_ref, dn1_ref, w_ref, *refs
):
    if not opening:
        (own_ref, above_ref, below_ref), refs = refs[:3], refs[3:]
    if closing:
        outs, (xs, state, res_ref, sems) = refs[:SUB], refs[SUB:]
    else:
        out_ref, edge_ref, xs, state = refs
    z, first, b = info_ref[0], info_ref[2], info_ref[3]
    clear_rims(xs, WIN)
    low_ok = jnp.where(z > 0, 1.0, 0.0)
    high_ok = jnp.where(z < 3, 1.0, 0.0)

    def put(buf, row, value):
        if row < BAND:
            value = value * low_ok
        elif row >= 2 * BAND:
            value = value * high_ok
        spread(xs, buf, row + 1, value)

    def begin():
        state[:BAND] = up0_ref[LEAD:].astype(f32)
        state[BAND : 2 * BAND] = v1_ref[...]
        state[2 * BAND :] = dn0_ref[LEAD:].astype(f32)

    def resume():
        state[:BAND] = above_ref[...].astype(f32)
        state[BAND : 2 * BAND] = own_ref[...]
        state[2 * BAND :] = below_ref[...].astype(f32)

    if opening:
        begin()
    else:
        pl.when(first == 1)(begin)
        pl.when(first == 0)(resume)

    for row in range(0, WIN, 2):
        put(0, row, state[row : row + 2].reshape(2 * C, W))

    for s, rows in enumerate(EDGE):
        now = s % 2
        half = s // SUB
        if closing:
            res_ref[FLOW * half + lax.rem(s // 2 % FLOW - b + FLOW, FLOW), now] = xs[now, BAND + 1 : 2 * BAND + 1, 1]
            if s == STEPS - 1:
                break
        matrix = banded([w_ref[s, t] for t in range(3)])
        up_ref, dn_ref = (up1_ref, dn1_ref) if half else (up0_ref, dn0_ref)
        for row in range(BAND - rows, 2 * BAND + rows, 4):
            for k, t in enumerate(block(xs, now, matrix, row)):
                r = row + 2 * k
                if r < BAND:
                    at = OFFSET[s] - half * LEAD + r - (BAND - rows)
                    d = up_ref[at : at + 2]
                elif r < 2 * BAND:
                    d = d_ref[s, r - BAND : r - BAND + 2]
                else:
                    at = OFFSET[s] - half * LEAD + r - 2 * BAND
                    d = dn_ref[at : at + 2]
                x = state[r : r + 2].reshape(2 * C, W) + ((M * H) * t + d.astype(f32).reshape(2 * C, W))
                state[r : r + 2] = x.reshape(2, C, W)
                if s < STEPS - 1:
                    put(1 - now, r, x)
    if closing:
        drain(res_ref, outs, sems)
    else:
        out_ref[...] = state[BAND : 2 * BAND]
        edge_ref[...] = state[BAND : 2 * BAND].astype(bf16)


VM = pl.BlockSpec(memory_space=pltpu.VMEM)
GRANT = pltpu.CompilerParams(vmem_limit_bytes=18 * 1024 * 1024)
SM = pl.BlockSpec(memory_space=pltpu.SMEM)
AN = pl.BlockSpec(memory_space=pl.ANY)


def shape(*dims, dtype=bf16):
    return jax.ShapeDtypeStruct(dims, dtype)


def relax(info, *arrays):
    outs = pl.pallas_call(
        relax_kernel,
        out_shape=(shape(CHUNK, C, W),) * FLOW + (shape(BAND, C, W, dtype=f32),),
        in_specs=[SM] + [VM] * 7,
        out_specs=(AN,) * FLOW + (VM,),
        scratch_shapes=[
            pltpu.VMEM((4, SPAN + 2, 3, C, W), bf16),
            pltpu.VMEM((2, SPAN, C, W), f32),
            pltpu.VMEM((2, BAND, C, W), f32),
            pltpu.VMEM((FLOW, CHUNK, C, W), bf16),
            pltpu.SemaphoreType.DMA((FLOW,)),
        ],
        compiler_params=GRANT,
        name="relax",
    )(info, *arrays)
    return outs[:FLOW], outs[FLOW]


def rims(half, b, *arrays):
    total = HALO - LEAD if half else LEAD + BAND
    return pl.pallas_call(
        functools.partial(rim_kernel, half),
        out_shape=(shape(total, C, W),) * 2,
        in_specs=[SM] + [VM] * len(arrays),
        out_specs=(VM, VM),
        scratch_shapes=[pltpu.VMEM((SUB, BAND, C, W), bf16)],
        compiler_params=GRANT,
    )(b, *arrays)


def finish(info, arrays):
    return pl.pallas_call(
        finish_kernel,
        out_shape=shape(2 * IMAGES * C * BAND, W, dtype=f32),
        in_specs=[SM] + [AN] * SUB,
        out_specs=VM,
        scratch_shapes=[
            pltpu.VMEM((IMAGES, 2, BAND, C, W), bf16),
            pltpu.VMEM((IMAGES, 2, BAND * C, W), f32),
            pltpu.SemaphoreType.DMA((IMAGES,)),
        ],
        compiler_params=GRANT,
        name="finish",
    )(info, *arrays)


def order(sub, chunks):
    return pl.pallas_call(
        order_kernel,
        out_shape=(shape(STEPS, BAND, C, W), shape(STEPS, 3, C, W)),
        in_specs=[SM] + [VM] * SUB,
        out_specs=(VM, VM),
        cost_estimate=pl.CostEstimate(flops=0, bytes_accessed=5_000_000, transcendentals=0),
        compiler_params=GRANT,
        name="order",
    )(sub, *chunks)


def sweep(opening, closing, info, *arrays):
    if closing:
        out_shape = (shape(2, BAND, C, W),) * SUB
        extra = [pltpu.VMEM((SUB, 2, BAND, C, W), bf16), pltpu.SemaphoreType.DMA((SUB,))]
    else:
        out_shape = (shape(BAND, C, W, dtype=f32), shape(BAND, C, W))
        extra = []
    return pl.pallas_call(
        functools.partial(sweep_kernel, opening, closing),
        out_shape=out_shape,
        in_specs=[SM] + [VM] * len(arrays),
        out_specs=(AN,) * SUB if closing else (VM, VM),
        scratch_shapes=[pltpu.VMEM((2, WIN + 2, 3, C, W), bf16), pltpu.VMEM((WIN, C, W), f32)] + extra,
        compiler_params=GRANT,
        name="sweep",
    )(info, *arrays)


def cycle(weights, image, guess):
    layers, rows = lax.axis_size("layer"), lax.axis_size("rows")
    groups = layers // SUB
    l, z = lax.axis_index("layer"), lax.axis_index("rows")
    sub, group = lax.rem(l, SUB), l // SUB
    mine = jnp.where(sub == home(1), 1, jnp.where(sub == home(2), 2, 0))

    own_image = lax.dynamic_index_in_dim(image, mine, 0, keepdims=False)
    flat = guess.reshape(2 * IMAGES, C, BAND, W)

    def edge_rows(first):
        rim = jnp.concatenate([flat[:, :, first : first + REACH], own_image[None, :, first : first + REACH]], axis=0)
        return rim.transpose(0, 2, 1, 3).astype(bf16)

    small = weights[:M]
    up = lax.ppermute(edge_rows(BAND - REACH), "rows", [(i, i + 1) for i in range(rows - 1)])
    dn = lax.ppermute(edge_rows(0), "rows", [(i + 1, i) for i in range(rows - 1)])
    following = lax.ppermute(small, "layer", [(i + 1, i) for i in range(layers - 1)])
    opening = small
    for b in range(1, IMAGES):
        got = lax.ppermute(small, "layer", [(0, home(b))])
        opening = jnp.where(l == home(b), got, opening)

    lead = jnp.where(group == 0, 1, 0)
    info = jnp.stack([z, lax.rem(sub, FLOW), lead, mine, sub // FLOW]).astype(jnp.int32)
    sends, v1 = relax(
        info, guess.reshape(-1, W), up, dn, own_image.reshape(-1, W), weights, following, opening
    )

    def pairs(half, k):
        return [
            (SUB * g + FLOW * half + (b + k) % FLOW, SUB * g + home(b))
            for g in range(groups)
            for b in range(IMAGES)
        ]

    received = [[lax.ppermute(sends[k], "layer", pairs(h, k)) for k in range(FLOW)] for h in range(HALVES)]

    def among_sweepers(value, ahead, by):
        pairs = []
        for g in range(groups - ahead):
            for b in range(IMAGES):
                for k in range(rows):
                    if 0 <= k + by < rows:
                        source = (SUB * g + home(b)) * rows + k
                        target = (SUB * (g + ahead) + home(b)) * rows + k + by
                        pairs.append((source, target))
        return lax.ppermute(value, ("layer", "rows"), pairs)

    images = mine.astype(jnp.int32).reshape(1)
    up, dn = rims(0, images, *received[0], v1)
    up0, dn0 = among_sweepers(up, 0, 1), among_sweepers(dn, 0, -1)
    up, dn = rims(1, images, *received[1])
    up1, dn1 = among_sweepers(up, 0, 1), among_sweepers(dn, 0, -1)
    d, w = order(images, received[0] + received[1])

    handed = ()
    for stage in range(groups - 1):
        state, edge = sweep(stage == 0, False, info, v1, d, up0, dn0, up1, dn1, w, *handed)
        handed = among_sweepers(state, 1, 0), among_sweepers(edge, 1, 1), among_sweepers(edge, 1, -1)
    results = sweep(False, True, info, v1, d, up0, dn0, up1, dn1, w, *handed)

    back = []
    for h in range(HALVES):
        for k in range(FLOW):
            back.append(lax.ppermute(results[FLOW * h + k], "layer", [(t, s) for s, t in pairs(h, k)]))
    return finish(info, back).reshape(guess.shape)


def solution(mesh):
    return jax.shard_map(
        cycle,
        mesh=mesh,
        in_specs=(
            P("layer", None, None),
            P(None, None, "rows", None),
            P("layer", None, None, "rows", None),
        ),
        out_specs=P("layer", None, None, "rows", None),
        check_vma=False,
    )
```

```python
import functools

import jax
import jax.numpy as jnp
from jax import lax
from jax.experimental import pallas as pl
from jax.experimental.pallas import tpu as pltpu
from jax.sharding import PartitionSpec as P


M = 4
H = 0.125
C = 32
W = 128
BAND = 16
SUB = 8
STEPS = 2 * SUB
IMAGES = 3
WIN = 3 * BAND
REACH = 4
SPAN = BAND + 2 * REACH
EDGE = [BAND - (s + 1) // 2 * 2 for s in range(STEPS)]
OFFSET = [sum(EDGE[:s]) for s in range(STEPS)]
HALO = sum(EDGE)
CHUNK = 2 * BAND + 6
bf16 = jnp.bfloat16
f32 = jnp.float32


FLOW = 4
HALVES = 2
LEAD = sum(EDGE[: STEPS // 2])


def home(b):
    return (0, 2, 6)[b]


def banded(tiles):
    lane = lax.broadcasted_iota(jnp.int32, (C, W), 1)
    keep = lane < 3 * C
    last, columns = jnp.zeros((C, W), bf16), []
    for tile in tiles:
        turned = pltpu.roll(tile, 3 * C, 1)
        columns.append(jnp.concatenate([tile, jnp.where(keep, last, turned)], axis=0))
        last = turned
    return jnp.concatenate(columns, axis=1)


def spread(xs, buf, row, value):
    lane = lax.broadcasted_iota(jnp.int32, (2 * C, W), 1)
    value = value.astype(bf16)
    left = jnp.where(lane == 0, bf16(0), pltpu.roll(value, 1, 1))
    right = jnp.where(lane == W - 1, bf16(0), pltpu.roll(value, W - 1, 1))
    for dc, v in enumerate((left, value, right)):
        xs[buf, row : row + 2, dc] = v.reshape(2, C, W)


def block(xs, buf, matrix, row):
    a = xs[buf, row : row + 4].reshape(12 * C, W)
    b = xs[buf, row + 2 : row + 6].reshape(12 * C, W)
    rhs = jnp.concatenate([a, b], axis=1)
    z = jnp.dot(matrix, rhs, preferred_element_type=f32)
    return jnp.tanh(z[:, :W]), jnp.tanh(z[:, W:])


def clear_rims(xs, rows):
    for buf in range(xs.shape[0]):
        for row in (0, rows + 1):
            xs[buf, row] = jnp.zeros((3, C, W), bf16)


def relaxer(info_ref, xs, state):
    low_ok = jnp.where(info_ref[0] > 0, 1.0, 0.0)
    high_ok = jnp.where(info_ref[0] < 3, 1.0, 0.0)

    def put(buf, row, value):
        if row < REACH:
            value = value * low_ok
        elif row >= REACH + BAND:
            value = value * high_ok
        spread(xs, buf, row + 1, value)

    def load(point, u, up_ref, own_ref, dn_ref, at):
        for r in range(0, SPAN, 2):
            if r < REACH:
                x = up_ref[u, r : r + 2]
            elif r >= REACH + BAND:
                x = dn_ref[u, r - REACH - BAND : r - REACH - BAND + 2]
            else:
                x = [own_ref[pl.ds(at + r - REACH + k, C, stride=BAND), :] for k in range(2)]
                x = jnp.concatenate(x, axis=0).astype(bf16)
            x = x.astype(f32).reshape(2 * C, W)
            state[point, r : r + 2] = x.reshape(2, C, W)
            put(2 * point, r, x)

    def layer(point, j, matrix, base=None):
        lo = (j + 1) // 2 * 2
        for row in range(lo, SPAN - lo, 4):
            for i, t in enumerate(block(xs, 2 * point + j % 2, matrix, row)):
                r = row + 2 * i
                x = state[point, r : r + 2].reshape(2 * C, W)
                if j == 0 and base is not None and REACH <= r < REACH + BAND:
                    base[point, r - REACH : r - REACH + 2] = (x + (M * H) * t).reshape(2, C, W)
                x = x + H * t
                state[point, r : r + 2] = x.reshape(2, C, W)
                if j < M - 1:
                    put(2 * point + (j + 1) % 2, r, x)

    return load, layer


def tiles(ref, n):
    tail = jnp.concatenate([ref[n, :, 2 * W :], jnp.zeros((C, 3 * C), bf16)], axis=1)
    return [ref[n, :, :W], ref[n, :, W : 2 * W], tail]


def drain(source, targets, sems):
    copies = [pltpu.make_async_copy(source.at[r], target, sems.at[r]) for r, target in enumerate(targets)]
    for copy in copies:
        copy.start()
    for copy in copies:
        copy.wait()


def relax_kernel(info_ref, own_ref, up_ref, dn_ref, here_ref, next_ref, *refs):
    outs, (xs, state, base, slots, sems) = refs[:FLOW], refs[FLOW:]
    load, layer = relaxer(info_ref, xs, state)
    clear_rims(xs, SPAN)

    def tap(point, j):
        return tiles(next_ref, j) if point else tiles(here_ref, M + j)

    def image(b, carry):
        for point in range(2):
            u = point * IMAGES + b
            load(point, u, up_ref, own_ref, dn_ref, u * (C * BAND))
        for j in range(M):
            for point in range(2):
                layer(point, j, banded(tap(point, j)), base)
        slot = lax.rem(info_ref[1] - b + FLOW, FLOW)
        for point in range(2):
            change = state[point, REACH : REACH + BAND] - base[point]
            slots[slot, point * BAND : (point + 1) * BAND] = change.astype(bf16)
            for t, tile in enumerate(tap(point, 0)):
                slots[slot, 2 * BAND + 3 * point + t] = tile
        return carry

    lax.fori_loop(0, IMAGES, image, 0)
    drain(slots, outs, sems)


def opening_kernel(info_ref, img_ref, up_ref, dn_ref, open_ref, v1_ref, xs, state):
    load, layer = relaxer(info_ref, xs, state)

    @pl.when(info_ref[2] == 1)
    def _():
        clear_rims(xs, SPAN)
        load(0, 2 * IMAGES, up_ref, img_ref, dn_ref, 0)
        for j in range(M):
            layer(0, j, banded(tiles(open_ref, j)))
        for r in range(BAND):
            x = img_ref[pl.ds(r, C, stride=BAND), :]
            v1_ref[r] = x + (state[0, REACH + r] - x.astype(bf16).astype(f32))


def rim_kernel(half, b_ref, *refs):
    chunks, rest = refs[:FLOW], refs[FLOW:]
    if half == 0:
        v1_ref, up_ref, dn_ref, d_ref = rest
        v1 = v1_ref[...].astype(bf16)
        up_ref[LEAD:] = v1
        dn_ref[LEAD:] = v1
    else:
        up_ref, dn_ref, d_ref = rest
    for k in range(FLOW):
        at = lax.rem(b_ref[0] + k, FLOW)
        for p in range(2):
            d_ref[2 * at + p] = chunks[k][p * BAND : (p + 1) * BAND]
    for s in range(SUB):
        rows, to = EDGE[SUB * half + s], OFFSET[SUB * half + s] - half * LEAD
        if rows:
            up_ref[to : to + rows] = d_ref[s, BAND - rows :]
            dn_ref[to : to + rows] = d_ref[s, :rows]


def order_kernel(b_ref, *refs):
    chunks, (d_ref, w_ref) = refs[:SUB], refs[SUB:]
    for r in range(SUB):
        at = SUB // 2 * (r // FLOW) + lax.rem(b_ref[0] + r % FLOW, FLOW)
        for p in range(2):
            d_ref[2 * at + p] = chunks[r][p * BAND : (p + 1) * BAND]
            w_ref[2 * at + p] = chunks[r][2 * BAND + 3 * p : 2 * BAND + 3 * p + 3]


def finish_kernel(info_ref, *refs):
    arrived, (out_ref, picked, stage, sems) = refs[:SUB], refs[SUB:]
    turn, half = info_ref[1], info_ref[4]
    for b in range(IMAGES):
        want = lax.rem(turn - b + FLOW, FLOW) + FLOW * half
        for r in range(SUB):

            @pl.when(want == r)
            def _():
                pltpu.make_async_copy(arrived[r], picked.at[b], sems.at[b]).start()

    for b in range(IMAGES):
        pltpu.make_async_copy(arrived[0], picked.at[b], sems.at[b]).wait()
        for p in range(2):
            stage[b, p] = picked[b, p].astype(f32).reshape(BAND * C, W)
            for c in range(C):
                to = ((p * IMAGES + b) * C + c) * BAND
                out_ref[to : to + BAND] = stage[b, p, pl.ds(c, BAND, stride=C), :]


def sweep_kernel(
    stage, closing, info_ref, v1_ref, d_ref, up0_ref, dn0_ref, up1_ref, dn1_ref, w_ref, *refs
):
    inputs = 3 * (stage if closing else min(stage, 1))
    handed, refs = refs[:inputs], refs[inputs:]
    if closing:
        outs, (xs, state, res_ref, sems) = refs[:SUB], refs[SUB:]
    else:
        out_ref, edge_ref, xs, state = refs
    z, b, group = info_ref[0], info_ref[3], info_ref[5]
    low_ok = jnp.where(z > 0, 1.0, 0.0)
    high_ok = jnp.where(z < 3, 1.0, 0.0)

    def put(buf, row, value):
        if row < BAND:
            value = value * low_ok
        elif row >= 2 * BAND:
            value = value * high_ok
        spread(xs, buf, row + 1, value)

    def begin():
        state[:BAND] = up0_ref[LEAD:].astype(f32)
        state[BAND : 2 * BAND] = v1_ref[...]
        state[2 * BAND :] = dn0_ref[LEAD:].astype(f32)

    def resume(own_ref, above_ref, below_ref):
        state[:BAND] = above_ref[...].astype(f32)
        state[BAND : 2 * BAND] = own_ref[...]
        state[2 * BAND :] = below_ref[...].astype(f32)

    def run():
        clear_rims(xs, WIN)
        if closing:
            pl.when(group == 0)(begin)
            for g in range(stage):
                pl.when(group == g + 1)(functools.partial(resume, *handed[3 * g : 3 * g + 3]))
        elif stage == 0:
            begin()
        else:
            resume(*handed)

        for row in range(0, WIN, 2):
            put(0, row, state[row : row + 2].reshape(2 * C, W))

        for s, rows in enumerate(EDGE):
            now = s % 2
            half = s // SUB
            if closing:
                res_ref[FLOW * half + lax.rem(s // 2 % FLOW - b + FLOW, FLOW), now] = xs[now, BAND + 1 : 2 * BAND + 1, 1]
                if s == STEPS - 1:
                    break
            matrix = banded([w_ref[s, t] for t in range(3)])
            up_ref, dn_ref = (up1_ref, dn1_ref) if half else (up0_ref, dn0_ref)
            for row in range(BAND - rows, 2 * BAND + rows, 4):
                for k, t in enumerate(block(xs, now, matrix, row)):
                    r = row + 2 * k
                    if r < BAND:
                        at = OFFSET[s] - half * LEAD + r - (BAND - rows)
                        d = up_ref[at : at + 2]
                    elif r < 2 * BAND:
                        d = d_ref[s, r - BAND : r - BAND + 2]
                    else:
                        at = OFFSET[s] - half * LEAD + r - 2 * BAND
                        d = dn_ref[at : at + 2]
                    x = state[r : r + 2].reshape(2 * C, W) + ((M * H) * t + d.astype(f32).reshape(2 * C, W))
                    state[r : r + 2] = x.reshape(2, C, W)
                    if s < STEPS - 1:
                        put(1 - now, r, x)
        if closing:
            drain(res_ref, outs, sems)
        else:
            out_ref[...] = state[BAND : 2 * BAND]
            edge_ref[...] = state[BAND : 2 * BAND].astype(bf16)

    if closing:
        run()
    else:
        pl.when(group == stage)(run)


VM = pl.BlockSpec(memory_space=pltpu.VMEM)
GRANT = pltpu.CompilerParams(vmem_limit_bytes=18 * 1024 * 1024)
SM = pl.BlockSpec(memory_space=pltpu.SMEM)
AN = pl.BlockSpec(memory_space=pl.ANY)


def shape(*dims, dtype=bf16):
    return jax.ShapeDtypeStruct(dims, dtype)


def relax(info, *arrays):
    return pl.pallas_call(
        relax_kernel,
        out_shape=(shape(CHUNK, C, W),) * FLOW,
        in_specs=[SM] + [VM] * len(arrays),
        out_specs=(AN,) * FLOW,
        scratch_shapes=[
            pltpu.VMEM((4, SPAN + 2, 3, C, W), bf16),
            pltpu.VMEM((2, SPAN, C, W), f32),
            pltpu.VMEM((2, BAND, C, W), f32),
            pltpu.VMEM((FLOW, CHUNK, C, W), bf16),
            pltpu.SemaphoreType.DMA((FLOW,)),
        ],
        compiler_params=GRANT,
        name="relax",
    )(info, *arrays)


def opened(info, *arrays):
    return pl.pallas_call(
        opening_kernel,
        out_shape=shape(BAND, C, W, dtype=f32),
        in_specs=[SM] + [VM] * len(arrays),
        out_specs=VM,
        scratch_shapes=[
            pltpu.VMEM((2, SPAN + 2, 3, C, W), bf16),
            pltpu.VMEM((1, SPAN, C, W), f32),
        ],
        compiler_params=GRANT,
        name="opening",
    )(info, *arrays)


def rims(half, b, *arrays):
    total = HALO - LEAD if half else LEAD + BAND
    return pl.pallas_call(
        functools.partial(rim_kernel, half),
        out_shape=(shape(total, C, W),) * 2,
        in_specs=[SM] + [VM] * len(arrays),
        out_specs=(VM, VM),
        scratch_shapes=[pltpu.VMEM((SUB, BAND, C, W), bf16)],
        compiler_params=GRANT,
    )(b, *arrays)


def finish(info, arrays):
    return pl.pallas_call(
        finish_kernel,
        out_shape=shape(2 * IMAGES * C * BAND, W, dtype=f32),
        in_specs=[SM] + [AN] * SUB,
        out_specs=VM,
        scratch_shapes=[
            pltpu.VMEM((IMAGES, 2, BAND, C, W), bf16),
            pltpu.VMEM((IMAGES, 2, BAND * C, W), f32),
            pltpu.SemaphoreType.DMA((IMAGES,)),
        ],
        compiler_params=GRANT,
        name="finish",
    )(info, *arrays)


def order(sub, chunks):
    return pl.pallas_call(
        order_kernel,
        out_shape=(shape(STEPS, BAND, C, W), shape(STEPS, 3, C, W)),
        in_specs=[SM] + [VM] * SUB,
        out_specs=(VM, VM),
        cost_estimate=pl.CostEstimate(flops=0, bytes_accessed=5_000_000, transcendentals=0),
        compiler_params=GRANT,
        name="order",
    )(sub, *chunks)


def sweep(stage, closing, info, *arrays):
    if closing:
        out_shape = (shape(2, BAND, C, W),) * SUB
        extra = [pltpu.VMEM((SUB, 2, BAND, C, W), bf16), pltpu.SemaphoreType.DMA((SUB,))]
    else:
        out_shape = (shape(BAND, C, W, dtype=f32), shape(BAND, C, W))
        extra = []
    return pl.pallas_call(
        functools.partial(sweep_kernel, stage, closing),
        out_shape=out_shape,
        in_specs=[SM] + [VM] * len(arrays),
        out_specs=(AN,) * SUB if closing else (VM, VM),
        scratch_shapes=[pltpu.VMEM((2, WIN + 2, 3, C, W), bf16), pltpu.VMEM((WIN, C, W), f32)] + extra,
        compiler_params=GRANT,
        name="sweep",
    )(info, *arrays)


def cycle(weights, image, guess):
    layers, rows = lax.axis_size("layer"), lax.axis_size("rows")
    groups = layers // SUB
    l, z = lax.axis_index("layer"), lax.axis_index("rows")
    sub, group = lax.rem(l, SUB), l // SUB
    mine = jnp.where(sub == home(1), 1, jnp.where(sub == home(2), 2, 0))

    own_image = lax.dynamic_index_in_dim(image, mine, 0, keepdims=False)
    flat = guess.reshape(2 * IMAGES, C, BAND, W)

    def edge_rows(first):
        rim = jnp.concatenate([flat[:, :, first : first + REACH], own_image[None, :, first : first + REACH]], axis=0)
        return rim.transpose(0, 2, 1, 3).astype(bf16)

    small = weights[:M]
    up = lax.ppermute(edge_rows(BAND - REACH), "rows", [(i, i + 1) for i in range(rows - 1)])
    dn = lax.ppermute(edge_rows(0), "rows", [(i + 1, i) for i in range(rows - 1)])
    following = lax.ppermute(small, "layer", [(i + 1, i) for i in range(layers - 1)])
    opening = small
    for b in range(1, IMAGES):
        got = lax.ppermute(small, "layer", [(0, home(b))])
        opening = jnp.where(l == home(b), got, opening)

    lead = jnp.where(group == 0, 1, 0)
    info = jnp.stack([z, lax.rem(sub, FLOW), lead, mine, sub // FLOW, group]).astype(jnp.int32)
    sends = relax(info, guess.reshape(-1, W), up, dn, weights, following)

    def pairs(half, k):
        return [
            (SUB * g + FLOW * half + (b + k) % FLOW, SUB * g + home(b))
            for g in range(groups)
            for b in range(IMAGES)
        ]

    received = [
        [lax.ppermute(sends[k], "layer", pairs(h, k)) for k in range(FLOW)] for h in range(HALVES)
    ]

    v1 = opened(info, own_image.reshape(-1, W), up, dn, opening)

    def among_sweepers(value, ahead, by, live):
        pairs = []
        for g in live:
            for b in range(IMAGES):
                for k in range(rows):
                    if 0 <= k + by < rows:
                        source = (SUB * g + home(b)) * rows + k
                        target = (SUB * (g + ahead) + home(b)) * rows + k + by
                        pairs.append((source, target))
        return lax.ppermute(value, ("layer", "rows"), pairs)

    images = mine.astype(jnp.int32).reshape(1)
    up, dn = rims(0, images, *received[0], v1)
    up0, dn0 = among_sweepers(up, 0, 1, range(groups)), among_sweepers(dn, 0, -1, range(groups))
    up, dn = rims(1, images, *received[1])
    up1, dn1 = among_sweepers(up, 0, 1, range(groups)), among_sweepers(dn, 0, -1, range(groups))
    d, w = order(images, received[0] + received[1])

    handed = []
    for stage in range(groups - 1):
        state, edge = sweep(stage, False, info, v1, d, up0, dn0, up1, dn1, w, *handed[-3:])
        for value, by in ((state, 0), (edge, 1), (edge, -1)):
            handed.append(among_sweepers(value, 1, by, [stage]))
    results = sweep(groups - 1, True, info, v1, d, up0, dn0, up1, dn1, w, *handed)

    back = []
    for h in range(HALVES):
        for k in range(FLOW):
            back.append(lax.ppermute(results[FLOW * h + k], "layer", [(t, s) for s, t in pairs(h, k)]))
    return finish(info, back).reshape(guess.shape)


def solution(mesh):
    return jax.shard_map(
        cycle,
        mesh=mesh,
        in_specs=(
            P("layer", None, None),
            P(None, None, "rows", None),
            P("layer", None, None, "rows", None),
        ),
        out_specs=P("layer", None, None, "rows", None),
        check_vma=False,
    )
```

```python
import functools

import jax
import jax.numpy as jnp
from jax import lax
from jax.experimental import pallas as pl
from jax.experimental.pallas import tpu as pltpu
from jax.sharding import PartitionSpec as P


M = 4
H = 0.125
C = 32
W = 128
BAND = 16
SUB = 8
STEPS = 2 * SUB
IMAGES = 3
WIN = 3 * BAND
REACH = 4
SPAN = BAND + 2 * REACH
EDGE = [BAND - (s + 1) // 2 * 2 for s in range(STEPS)]
OFFSET = [sum(EDGE[:s]) for s in range(STEPS)]
HALO = sum(EDGE)
CHUNK = 2 * BAND + 6
bf16 = jnp.bfloat16
f32 = jnp.float32


FLOW = 4
HALVES = 2
LEAD = sum(EDGE[: STEPS // 2])


def home(b):
    return (0, 2, 6)[b]


def banded(tiles):
    lane = lax.broadcasted_iota(jnp.int32, (C, W), 1)
    keep = lane < 3 * C
    last, columns = jnp.zeros((C, W), bf16), []
    for tile in tiles:
        turned = pltpu.roll(tile, 3 * C, 1)
        columns.append(jnp.concatenate([tile, jnp.where(keep, last, turned)], axis=0))
        last = turned
    return jnp.concatenate(columns, axis=1)


def spread(xs, buf, row, value):
    lane = lax.broadcasted_iota(jnp.int32, (2 * C, W), 1)
    value = value.astype(bf16)
    left = jnp.where(lane == 0, bf16(0), pltpu.roll(value, 1, 1))
    right = jnp.where(lane == W - 1, bf16(0), pltpu.roll(value, W - 1, 1))
    for dc, v in enumerate((left, value, right)):
        xs[buf, row : row + 2, dc] = v.reshape(2, C, W)


def block(xs, buf, matrix, row):
    a = xs[buf, row : row + 4].reshape(12 * C, W)
    b = xs[buf, row + 2 : row + 6].reshape(12 * C, W)
    rhs = jnp.concatenate([a, b], axis=1)
    z = jnp.dot(matrix, rhs, preferred_element_type=f32)
    return jnp.tanh(z[:, :W]), jnp.tanh(z[:, W:])


def clear_rims(xs, rows):
    for buf in range(xs.shape[0]):
        for row in (0, rows + 1):
            xs[buf, row] = jnp.zeros((3, C, W), bf16)


def relaxer(info_ref, xs, state):
    low_ok = jnp.where(info_ref[0] > 0, 1.0, 0.0)
    high_ok = jnp.where(info_ref[0] < 3, 1.0, 0.0)

    def put(buf, row, value):
        if row < REACH:
            value = value * low_ok
        elif row >= REACH + BAND:
            value = value * high_ok
        spread(xs, buf, row + 1, value)

    def load(point, u, up_ref, own_ref, dn_ref, at):
        for r in range(0, SPAN, 2):
            if r < REACH:
                x = up_ref[u, r : r + 2]
            elif r >= REACH + BAND:
                x = dn_ref[u, r - REACH - BAND : r - REACH - BAND + 2]
            else:
                x = [own_ref[pl.ds(at + r - REACH + k, C, stride=BAND), :] for k in range(2)]
                x = jnp.concatenate(x, axis=0).astype(bf16)
            x = x.astype(f32).reshape(2 * C, W)
            state[point, r : r + 2] = x.reshape(2, C, W)
            put(2 * point, r, x)

    def layer(point, j, matrix, base=None):
        lo = (j + 1) // 2 * 2
        for row in range(lo, SPAN - lo, 4):
            for i, t in enumerate(block(xs, 2 * point + j % 2, matrix, row)):
                r = row + 2 * i
                x = state[point, r : r + 2].reshape(2 * C, W)
                if j == 0 and base is not None and REACH <= r < REACH + BAND:
                    base[point, r - REACH : r - REACH + 2] = (x + (M * H) * t).reshape(2, C, W)
                x = x + H * t
                state[point, r : r + 2] = x.reshape(2, C, W)
                if j < M - 1:
                    put(2 * point + (j + 1) % 2, r, x)

    return load, layer


def tiles(ref, n):
    tail = jnp.concatenate([ref[n, :, 2 * W :], jnp.zeros((C, 3 * C), bf16)], axis=1)
    return [ref[n, :, :W], ref[n, :, W : 2 * W], tail]


def drain(source, targets, sems):
    copies = [pltpu.make_async_copy(source.at[r], target, sems.at[r]) for r, target in enumerate(targets)]
    for copy in copies:
        copy.start()
    for copy in copies:
        copy.wait()


def relax_kernel(info_ref, own_ref, up_ref, dn_ref, here_ref, next_ref, *refs):
    outs, (xs, state, base, slots, sems) = refs[:FLOW], refs[FLOW:]
    load, layer = relaxer(info_ref, xs, state)
    clear_rims(xs, SPAN)

    def tap(point, j):
        return tiles(next_ref, j) if point else tiles(here_ref, M + j)

    def image(b, carry):
        for point in range(2):
            u = point * IMAGES + b
            load(point, u, up_ref, own_ref, dn_ref, u * (C * BAND))
        for j in range(M):
            for point in range(2):
                layer(point, j, banded(tap(point, j)), base)
        slot = lax.rem(info_ref[1] - b + FLOW, FLOW)
        for point in range(2):
            change = state[point, REACH : REACH + BAND] - base[point]
            slots[slot, point * BAND : (point + 1) * BAND] = change.astype(bf16)
            for t, tile in enumerate(tap(point, 0)):
                slots[slot, 2 * BAND + 3 * point + t] = tile
        return carry

    lax.fori_loop(0, IMAGES, image, 0)
    drain(slots, outs, sems)


def opening_kernel(info_ref, img_ref, up_ref, dn_ref, open_ref, v1_ref, xs, state):
    load, layer = relaxer(info_ref, xs, state)

    @pl.when(info_ref[2] == 1)
    def _():
        clear_rims(xs, SPAN)
        load(0, 2 * IMAGES, up_ref, img_ref, dn_ref, 0)
        for j in range(M):
            layer(0, j, banded(tiles(open_ref, j)))
        for r in range(BAND):
            x = img_ref[pl.ds(r, C, stride=BAND), :]
            v1_ref[r] = x + (state[0, REACH + r] - x.astype(bf16).astype(f32))


def rim_kernel(half, b_ref, *refs):
    chunks, rest = refs[:FLOW], refs[FLOW:]
    if half == 1:
        v1_ref, up_ref, dn_ref, d_ref = rest
        v1 = v1_ref[...].astype(bf16)
        up_ref[HALO - LEAD :] = v1
        dn_ref[HALO - LEAD :] = v1
    else:
        up_ref, dn_ref, d_ref = rest
    for k in range(FLOW):
        at = lax.rem(b_ref[0] + k, FLOW)
        for p in range(2):
            d_ref[2 * at + p] = chunks[k][p * BAND : (p + 1) * BAND]
    for s in range(SUB):
        rows, to = EDGE[SUB * half + s], OFFSET[SUB * half + s] - half * LEAD
        if rows:
            up_ref[to : to + rows] = d_ref[s, BAND - rows :]
            dn_ref[to : to + rows] = d_ref[s, :rows]


def order_kernel(b_ref, *refs):
    chunks, (d_ref, w_ref) = refs[:SUB], refs[SUB:]
    for r in range(SUB):
        at = SUB // 2 * (r // FLOW) + lax.rem(b_ref[0] + r % FLOW, FLOW)
        for p in range(2):
            d_ref[2 * at + p] = chunks[r][p * BAND : (p + 1) * BAND]
            w_ref[2 * at + p] = chunks[r][2 * BAND + 3 * p : 2 * BAND + 3 * p + 3]


def finish_kernel(info_ref, *refs):
    arrived, (out_ref, picked, stage, sems) = refs[:SUB], refs[SUB:]
    turn, half = info_ref[1], info_ref[4]
    for b in range(IMAGES):
        want = lax.rem(turn - b + FLOW, FLOW) + FLOW * half
        for r in range(SUB):

            @pl.when(want == r)
            def _():
                pltpu.make_async_copy(arrived[r], picked.at[b], sems.at[b]).start()

    for b in range(IMAGES):
        pltpu.make_async_copy(arrived[0], picked.at[b], sems.at[b]).wait()
        for p in range(2):
            stage[b, p] = picked[b, p].astype(f32).reshape(BAND * C, W)
            for c in range(C):
                to = ((p * IMAGES + b) * C + c) * BAND
                out_ref[to : to + BAND] = stage[b, p, pl.ds(c, BAND, stride=C), :]


def sweep_kernel(
    stage, closing, info_ref, v1_ref, d_ref, up0_ref, dn0_ref, up1_ref, dn1_ref, w_ref, *refs
):
    inputs = 3 * (stage if closing else min(stage, 1))
    handed, refs = refs[:inputs], refs[inputs:]
    if closing:
        outs, (xs, state, res_ref, sems) = refs[:SUB], refs[SUB:]
    else:
        out_ref, edge_ref, xs, state = refs
    z, b, group = info_ref[0], info_ref[3], info_ref[5]
    low_ok = jnp.where(z > 0, 1.0, 0.0)
    high_ok = jnp.where(z < 3, 1.0, 0.0)

    def put(buf, row, value):
        if row < BAND:
            value = value * low_ok
        elif row >= 2 * BAND:
            value = value * high_ok
        spread(xs, buf, row + 1, value)

    def begin():
        state[:BAND] = up1_ref[HALO - LEAD :].astype(f32)
        state[BAND : 2 * BAND] = v1_ref[...]
        state[2 * BAND :] = dn1_ref[HALO - LEAD :].astype(f32)

    def resume(own_ref, above_ref, below_ref):
        state[:BAND] = above_ref[...].astype(f32)
        state[BAND : 2 * BAND] = own_ref[...]
        state[2 * BAND :] = below_ref[...].astype(f32)

    def run():
        clear_rims(xs, WIN)
        if closing:
            pl.when(group == 0)(begin)
            for g in range(stage):
                pl.when(group == g + 1)(functools.partial(resume, *handed[3 * g : 3 * g + 3]))
        elif stage == 0:
            begin()
        else:
            resume(*handed)

        for row in range(0, WIN, 2):
            put(0, row, state[row : row + 2].reshape(2 * C, W))

        for s, rows in enumerate(EDGE):
            now = s % 2
            half = s // SUB
            if closing:
                res_ref[FLOW * half + lax.rem(s // 2 % FLOW - b + FLOW, FLOW), now] = xs[now, BAND + 1 : 2 * BAND + 1, 1]
                if s == STEPS - 1:
                    break
            matrix = banded([w_ref[s, t] for t in range(3)])
            up_ref, dn_ref = (up1_ref, dn1_ref) if half else (up0_ref, dn0_ref)
            for row in range(BAND - rows, 2 * BAND + rows, 4):
                for k, t in enumerate(block(xs, now, matrix, row)):
                    r = row + 2 * k
                    if r < BAND:
                        at = OFFSET[s] - half * LEAD + r - (BAND - rows)
                        d = up_ref[at : at + 2]
                    elif r < 2 * BAND:
                        d = d_ref[s, r - BAND : r - BAND + 2]
                    else:
                        at = OFFSET[s] - half * LEAD + r - 2 * BAND
                        d = dn_ref[at : at + 2]
                    x = state[r : r + 2].reshape(2 * C, W) + ((M * H) * t + d.astype(f32).reshape(2 * C, W))
                    state[r : r + 2] = x.reshape(2, C, W)
                    if s < STEPS - 1:
                        put(1 - now, r, x)
        if closing:
            drain(res_ref, outs, sems)
        else:
            out_ref[...] = state[BAND : 2 * BAND]
            edge_ref[...] = state[BAND : 2 * BAND].astype(bf16)

    if closing:
        run()
    else:
        pl.when(group == stage)(run)


VM = pl.BlockSpec(memory_space=pltpu.VMEM)
GRANT = pltpu.CompilerParams(vmem_limit_bytes=18 * 1024 * 1024)
SM = pl.BlockSpec(memory_space=pltpu.SMEM)
AN = pl.BlockSpec(memory_space=pl.ANY)


def shape(*dims, dtype=bf16):
    return jax.ShapeDtypeStruct(dims, dtype)


def relax(info, *arrays):
    return pl.pallas_call(
        relax_kernel,
        out_shape=(shape(CHUNK, C, W),) * FLOW,
        in_specs=[SM] + [VM] * len(arrays),
        out_specs=(AN,) * FLOW,
        scratch_shapes=[
            pltpu.VMEM((4, SPAN + 2, 3, C, W), bf16),
            pltpu.VMEM((2, SPAN, C, W), f32),
            pltpu.VMEM((2, BAND, C, W), f32),
            pltpu.VMEM((FLOW, CHUNK, C, W), bf16),
            pltpu.SemaphoreType.DMA((FLOW,)),
        ],
        compiler_params=GRANT,
        name="relax",
    )(info, *arrays)


def opened(info, *arrays):
    return pl.pallas_call(
        opening_kernel,
        out_shape=shape(BAND, C, W, dtype=f32),
        in_specs=[SM] + [VM] * len(arrays),
        out_specs=VM,
        scratch_shapes=[
            pltpu.VMEM((2, SPAN + 2, 3, C, W), bf16),
            pltpu.VMEM((1, SPAN, C, W), f32),
        ],
        compiler_params=GRANT,
        name="opening",
    )(info, *arrays)


def rims(half, b, *arrays):
    total = HALO - LEAD + BAND if half else LEAD
    return pl.pallas_call(
        functools.partial(rim_kernel, half),
        out_shape=(shape(total, C, W),) * 2,
        in_specs=[SM] + [VM] * len(arrays),
        out_specs=(VM, VM),
        scratch_shapes=[pltpu.VMEM((SUB, BAND, C, W), bf16)],
        compiler_params=GRANT,
    )(b, *arrays)


def finish(info, arrays):
    return pl.pallas_call(
        finish_kernel,
        out_shape=shape(2 * IMAGES * C * BAND, W, dtype=f32),
        in_specs=[SM] + [AN] * SUB,
        out_specs=VM,
        scratch_shapes=[
            pltpu.VMEM((IMAGES, 2, BAND, C, W), bf16),
            pltpu.VMEM((IMAGES, 2, BAND * C, W), f32),
            pltpu.SemaphoreType.DMA((IMAGES,)),
        ],
        compiler_params=GRANT,
        name="finish",
    )(info, *arrays)


def order(sub, chunks):
    return pl.pallas_call(
        order_kernel,
        out_shape=(shape(STEPS, BAND, C, W), shape(STEPS, 3, C, W)),
        in_specs=[SM] + [VM] * SUB,
        out_specs=(VM, VM),
        cost_estimate=pl.CostEstimate(flops=0, bytes_accessed=5_000_000, transcendentals=0),
        compiler_params=GRANT,
        name="order",
    )(sub, *chunks)


def sweep(stage, closing, info, *arrays):
    if closing:
        out_shape = (shape(2, BAND, C, W),) * SUB
        extra = [pltpu.VMEM((SUB, 2, BAND, C, W), bf16), pltpu.SemaphoreType.DMA((SUB,))]
    else:
        out_shape = (shape(BAND, C, W, dtype=f32), shape(BAND, C, W))
        extra = []
    return pl.pallas_call(
        functools.partial(sweep_kernel, stage, closing),
        out_shape=out_shape,
        in_specs=[SM] + [VM] * len(arrays),
        out_specs=(AN,) * SUB if closing else (VM, VM),
        scratch_shapes=[pltpu.VMEM((2, WIN + 2, 3, C, W), bf16), pltpu.VMEM((WIN, C, W), f32)] + extra,
        compiler_params=GRANT,
        name="sweep",
    )(info, *arrays)


def cycle(weights, image, guess):
    layers, rows = lax.axis_size("layer"), lax.axis_size("rows")
    groups = layers // SUB
    l, z = lax.axis_index("layer"), lax.axis_index("rows")
    sub, group = lax.rem(l, SUB), l // SUB
    mine = jnp.where(sub == home(1), 1, jnp.where(sub == home(2), 2, 0))

    own_image = lax.dynamic_index_in_dim(image, mine, 0, keepdims=False)
    flat = guess.reshape(2 * IMAGES, C, BAND, W)

    def edge_rows(first):
        rim = jnp.concatenate([flat[:, :, first : first + REACH], own_image[None, :, first : first + REACH]], axis=0)
        return rim.transpose(0, 2, 1, 3).astype(bf16)

    small = weights[:M]
    up = lax.ppermute(edge_rows(BAND - REACH), "rows", [(i, i + 1) for i in range(rows - 1)])
    dn = lax.ppermute(edge_rows(0), "rows", [(i + 1, i) for i in range(rows - 1)])
    following = lax.ppermute(small, "layer", [(i + 1, i) for i in range(layers - 1)])
    opening = small
    for b in range(1, IMAGES):
        got = lax.ppermute(small, "layer", [(0, home(b))])
        opening = jnp.where(l == home(b), got, opening)

    lead = jnp.where(group == 0, 1, 0)
    info = jnp.stack([z, lax.rem(sub, FLOW), lead, mine, sub // FLOW, group]).astype(jnp.int32)
    sends = relax(info, guess.reshape(-1, W), up, dn, weights, following)

    def pairs(half, k):
        return [
            (SUB * g + FLOW * half + (b + k) % FLOW, SUB * g + home(b))
            for g in range(groups)
            for b in range(IMAGES)
        ]

    received = [
        [lax.ppermute(sends[k], "layer", pairs(h, k)) for k in range(FLOW)] for h in range(HALVES)
    ]

    v1 = opened(info, own_image.reshape(-1, W), up, dn, opening)

    def among_sweepers(value, ahead, by, live):
        pairs = []
        for g in live:
            for b in range(IMAGES):
                for k in range(rows):
                    if 0 <= k + by < rows:
                        source = (SUB * g + home(b)) * rows + k
                        target = (SUB * (g + ahead) + home(b)) * rows + k + by
                        pairs.append((source, target))
        return lax.ppermute(value, ("layer", "rows"), pairs)

    images = mine.astype(jnp.int32).reshape(1)
    up, dn = rims(0, images, *received[0])
    up0 = among_sweepers(up, 0, 1, range(groups))
    dn0 = among_sweepers(dn, 0, -1, range(groups))
    up, dn = rims(1, images, *received[1], v1)
    up1, dn1 = among_sweepers(up, 0, 1, range(groups)), among_sweepers(dn, 0, -1, range(groups))
    d, w = order(images, received[0] + received[1])

    handed = []
    for stage in range(groups - 1):
        state, edge = sweep(stage, False, info, v1, d, up0, dn0, up1, dn1, w, *handed[-3:])
        for value, by in ((state, 0), (edge, 1), (edge, -1)):
            handed.append(among_sweepers(value, 1, by, [stage]))
    results = sweep(groups - 1, True, info, v1, d, up0, dn0, up1, dn1, w, *handed)

    back = []
    for h in range(HALVES):
        for k in range(FLOW):
            back.append(lax.ppermute(results[FLOW * h + k], "layer", [(t, s) for s, t in pairs(h, k)]))
    return finish(info, back).reshape(guess.shape)


def solution(mesh):
    return jax.shard_map(
        cycle,
        mesh=mesh,
        in_specs=(
            P("layer", None, None),
            P(None, None, "rows", None),
            P("layer", None, None, "rows", None),
        ),
        out_specs=P("layer", None, None, "rows", None),
        check_vma=False,
    )
```

```python
import functools

import jax
import jax.numpy as jnp
from jax import lax
from jax.experimental import pallas as pl
from jax.experimental.pallas import tpu as pltpu
from jax.sharding import PartitionSpec as P


M = 4
H = 0.125
C = 32
W = 128
BAND = 16
SUB = 8
STEPS = 2 * SUB
IMAGES = 3
WIN = 3 * BAND
REACH = 4
SPAN = BAND + 2 * REACH
EDGE = [BAND - (s + 1) // 2 * 2 for s in range(STEPS)]
OFFSET = [sum(EDGE[:s]) for s in range(STEPS)]
HALO = sum(EDGE)
CHUNK = 2 * BAND + 6
bf16 = jnp.bfloat16
f32 = jnp.float32


FLOW = 4
HALVES = 2
LEAD = sum(EDGE[: STEPS // 2])


def home(b):
    return (0, 2, 6)[b]


def banded(tiles):
    lane = lax.broadcasted_iota(jnp.int32, (C, W), 1)
    keep = lane < 3 * C
    last, columns = jnp.zeros((C, W), bf16), []
    for tile in tiles:
        turned = pltpu.roll(tile, 3 * C, 1)
        columns.append(jnp.concatenate([tile, jnp.where(keep, last, turned)], axis=0))
        last = turned
    return jnp.concatenate(columns, axis=1)


def spread(xs, buf, row, value):
    lane = lax.broadcasted_iota(jnp.int32, (2 * C, W), 1)
    value = value.astype(bf16)
    left = jnp.where(lane == 0, bf16(0), pltpu.roll(value, 1, 1))
    right = jnp.where(lane == W - 1, bf16(0), pltpu.roll(value, W - 1, 1))
    for dc, v in enumerate((left, value, right)):
        xs[buf, row : row + 2, dc] = v.reshape(2, C, W)


def block(xs, buf, matrix, row):
    a = xs[buf, row : row + 4].reshape(12 * C, W)
    b = xs[buf, row + 2 : row + 6].reshape(12 * C, W)
    rhs = jnp.concatenate([a, b], axis=1)
    z = jnp.dot(matrix, rhs, preferred_element_type=f32)
    return jnp.tanh(z[:, :W]), jnp.tanh(z[:, W:])


def clear_rims(xs, rows):
    for buf in range(xs.shape[0]):
        for row in (0, rows + 1):
            xs[buf, row] = jnp.zeros((3, C, W), bf16)


def relaxer(info_ref, xs, state):
    low_ok = jnp.where(info_ref[0] > 0, 1.0, 0.0)
    high_ok = jnp.where(info_ref[0] < 3, 1.0, 0.0)

    def put(buf, row, value):
        if row < REACH:
            value = value * low_ok
        elif row >= REACH + BAND:
            value = value * high_ok
        spread(xs, buf, row + 1, value)

    def load(point, u, up_ref, own_ref, dn_ref, at):
        for r in range(0, SPAN, 2):
            if r < REACH:
                x = up_ref[u, r : r + 2]
            elif r >= REACH + BAND:
                x = dn_ref[u, r - REACH - BAND : r - REACH - BAND + 2]
            else:
                x = [own_ref[pl.ds(at + r - REACH + k, C, stride=BAND), :] for k in range(2)]
                x = jnp.concatenate(x, axis=0).astype(bf16)
            x = x.astype(f32).reshape(2 * C, W)
            state[point, r : r + 2] = x.reshape(2, C, W)
            put(2 * point, r, x)

    def layer(point, j, matrix, base=None):
        lo = (j + 1) // 2 * 2
        for row in range(lo, SPAN - lo, 4):
            for i, t in enumerate(block(xs, 2 * point + j % 2, matrix, row)):
                r = row + 2 * i
                x = state[point, r : r + 2].reshape(2 * C, W)
                if j == 0 and base is not None and REACH <= r < REACH + BAND:
                    base[point, r - REACH : r - REACH + 2] = (x + (M * H) * t).reshape(2, C, W)
                x = x + H * t
                state[point, r : r + 2] = x.reshape(2, C, W)
                if j < M - 1:
                    put(2 * point + (j + 1) % 2, r, x)

    return load, layer


def edges_kernel(info_ref, own_ref, img_ref, up_ref, dn_ref):
    for u in range(2 * IMAGES + 1):
        ref, at = (own_ref, u * (C * BAND)) if u < 2 * IMAGES else (img_ref, info_ref[3] * (C * BAND))
        for r in range(REACH):
            dn_ref[u, r] = ref[pl.ds(at + r, C, stride=BAND), :].astype(bf16)
            up_ref[u, r] = ref[pl.ds(at + BAND - REACH + r, C, stride=BAND), :].astype(bf16)


def tiles(ref, n):
    tail = jnp.concatenate([ref[n, :, 2 * W :], jnp.zeros((C, 3 * C), bf16)], axis=1)
    return [ref[n, :, :W], ref[n, :, W : 2 * W], tail]


def drain(source, targets, sems):
    copies = [pltpu.make_async_copy(source.at[r], target, sems.at[r]) for r, target in enumerate(targets)]
    for copy in copies:
        copy.start()
    for copy in copies:
        copy.wait()


def relax_kernel(info_ref, own_ref, up_ref, dn_ref, here_ref, next_ref, *refs):
    outs, (xs, state, base, slots, sems) = refs[:FLOW], refs[FLOW:]
    load, layer = relaxer(info_ref, xs, state)
    clear_rims(xs, SPAN)

    def tap(point, j):
        return tiles(next_ref, j) if point else tiles(here_ref, M + j)

    def image(b, carry):
        for point in range(2):
            u = point * IMAGES + b
            load(point, u, up_ref, own_ref, dn_ref, u * (C * BAND))
        for j in range(M):
            for point in range(2):
                layer(point, j, banded(tap(point, j)), base)
        slot = lax.rem(info_ref[1] - b + FLOW, FLOW)
        for point in range(2):
            change = state[point, REACH : REACH + BAND] - base[point]
            slots[slot, point * BAND : (point + 1) * BAND] = change.astype(bf16)
            for t, tile in enumerate(tap(point, 0)):
                slots[slot, 2 * BAND + 3 * point + t] = tile
        return carry

    lax.fori_loop(0, IMAGES, image, 0)
    drain(slots, outs, sems)


def opening_kernel(info_ref, img_ref, up_ref, dn_ref, open_ref, v1_ref, xs, state):
    load, layer = relaxer(info_ref, xs, state)

    @pl.when(info_ref[2] == 1)
    def _():
        clear_rims(xs, SPAN)
        at = info_ref[3] * (C * BAND)
        load(0, 2 * IMAGES, up_ref, img_ref, dn_ref, at)
        for j in range(M):
            layer(0, j, banded(tiles(open_ref, j)))
        for r in range(BAND):
            x = img_ref[pl.ds(at + r, C, stride=BAND), :]
            v1_ref[r] = x + (state[0, REACH + r] - x.astype(bf16).astype(f32))


def rim_kernel(half, b_ref, *refs):
    chunks, rest = refs[:FLOW], refs[FLOW:]
    if half == 0:
        v1_ref, up_ref, dn_ref, d_ref = rest
        v1 = v1_ref[...].astype(bf16)
        up_ref[LEAD:] = v1
        dn_ref[LEAD:] = v1
    else:
        up_ref, dn_ref, d_ref = rest
    for k in range(FLOW):
        at = lax.rem(b_ref[0] + k, FLOW)
        for p in range(2):
            d_ref[2 * at + p] = chunks[k][p * BAND : (p + 1) * BAND]
    for s in range(SUB):
        rows, to = EDGE[SUB * half + s], OFFSET[SUB * half + s] - half * LEAD
        if rows:
            up_ref[to : to + rows] = d_ref[s, BAND - rows :]
            dn_ref[to : to + rows] = d_ref[s, :rows]


def order_kernel(b_ref, *refs):
    chunks, (d_ref, w_ref) = refs[:SUB], refs[SUB:]
    for r in range(SUB):
        at = SUB // 2 * (r // FLOW) + lax.rem(b_ref[0] + r % FLOW, FLOW)
        for p in range(2):
            d_ref[2 * at + p] = chunks[r][p * BAND : (p + 1) * BAND]
            w_ref[2 * at + p] = chunks[r][2 * BAND + 3 * p : 2 * BAND + 3 * p + 3]


def finish_kernel(info_ref, *refs):
    arrived, (out_ref, picked, stage, ready, sems, leave) = refs[:SUB], refs[SUB:]
    writes = []
    turn, half = info_ref[1], info_ref[4]
    for b in range(IMAGES):
        want = lax.rem(turn - b + FLOW, FLOW) + FLOW * half
        for r in range(SUB):

            @pl.when(want == r)
            def _():
                pltpu.make_async_copy(arrived[r], picked.at[b], sems.at[b]).start()

    for b in range(IMAGES):
        pltpu.make_async_copy(arrived[0], picked.at[b], sems.at[b]).wait()
        for p in range(2):
            stage[b, p] = picked[b, p].astype(f32).reshape(BAND * C, W)
            for c in range(C):
                ready[b, p, c * BAND : (c + 1) * BAND] = stage[b, p, pl.ds(c, BAND, stride=C), :]
            to = (p * IMAGES + b) * (C * BAND)
            copy = pltpu.make_async_copy(ready.at[b, p], out_ref.at[to : to + C * BAND], leave.at[b, p])
            copy.start()
            writes.append(copy)
    for copy in writes:
        copy.wait()


def sweep_kernel(
    stage, closing, info_ref, v1_ref, d_ref, up0_ref, dn0_ref, up1_ref, dn1_ref, w_ref, *refs
):
    inputs = 3 * (stage if closing else min(stage, 1))
    handed, refs = refs[:inputs], refs[inputs:]
    if closing:
        outs, (xs, state, res_ref, sems) = refs[:SUB], refs[SUB:]
    else:
        out_ref, edge_ref, xs, state = refs
    z, b, group = info_ref[0], info_ref[3], info_ref[5]
    low_ok = jnp.where(z > 0, 1.0, 0.0)
    high_ok = jnp.where(z < 3, 1.0, 0.0)

    def put(buf, row, value):
        if row < BAND:
            value = value * low_ok
        elif row >= 2 * BAND:
            value = value * high_ok
        spread(xs, buf, row + 1, value)

    def begin():
        state[:BAND] = up0_ref[LEAD:].astype(f32)
        state[BAND : 2 * BAND] = v1_ref[...]
        state[2 * BAND :] = dn0_ref[LEAD:].astype(f32)

    def resume(own_ref, above_ref, below_ref):
        state[:BAND] = above_ref[...].astype(f32)
        state[BAND : 2 * BAND] = own_ref[...]
        state[2 * BAND :] = below_ref[...].astype(f32)

    def run():
        clear_rims(xs, WIN)
        if closing:
            pl.when(group == 0)(begin)
            for g in range(stage):
                pl.when(group == g + 1)(functools.partial(resume, *handed[3 * g : 3 * g + 3]))
        elif stage == 0:
            begin()
        else:
            resume(*handed)

        for row in range(0, WIN, 2):
            put(0, row, state[row : row + 2].reshape(2 * C, W))

        for s, rows in enumerate(EDGE):
            now = s % 2
            half = s // SUB
            if closing:
                res_ref[FLOW * half + lax.rem(s // 2 % FLOW - b + FLOW, FLOW), now] = xs[now, BAND + 1 : 2 * BAND + 1, 1]
                if s == STEPS - 1:
                    break
            matrix = banded([w_ref[s, t] for t in range(3)])
            up_ref, dn_ref = (up1_ref, dn1_ref) if half else (up0_ref, dn0_ref)
            for row in range(BAND - rows, 2 * BAND + rows, 4):
                for k, t in enumerate(block(xs, now, matrix, row)):
                    r = row + 2 * k
                    if r < BAND:
                        at = OFFSET[s] - half * LEAD + r - (BAND - rows)
                        d = up_ref[at : at + 2]
                    elif r < 2 * BAND:
                        d = d_ref[s, r - BAND : r - BAND + 2]
                    else:
                        at = OFFSET[s] - half * LEAD + r - 2 * BAND
                        d = dn_ref[at : at + 2]
                    x = state[r : r + 2].reshape(2 * C, W) + ((M * H) * t + d.astype(f32).reshape(2 * C, W))
                    state[r : r + 2] = x.reshape(2, C, W)
                    if s < STEPS - 1:
                        put(1 - now, r, x)
        if closing:
            drain(res_ref, outs, sems)
        else:
            out_ref[...] = state[BAND : 2 * BAND]
            edge_ref[...] = state[BAND : 2 * BAND].astype(bf16)

    if closing:
        run()
    else:
        pl.when(group == stage)(run)


VM = pl.BlockSpec(memory_space=pltpu.VMEM)
GRANT = pltpu.CompilerParams(vmem_limit_bytes=18 * 1024 * 1024)
SM = pl.BlockSpec(memory_space=pltpu.SMEM)
AN = pl.BlockSpec(memory_space=pl.ANY)


def shape(*dims, dtype=bf16):
    return jax.ShapeDtypeStruct(dims, dtype)


def edges(info, *arrays):
    return pl.pallas_call(
        edges_kernel,
        out_shape=(shape(2 * IMAGES + 1, REACH, C, W),) * 2,
        in_specs=[SM] + [VM] * len(arrays),
        out_specs=(VM, VM),
        compiler_params=GRANT,
        name="edges",
    )(info, *arrays)


def relax(info, *arrays):
    return pl.pallas_call(
        relax_kernel,
        out_shape=(shape(CHUNK, C, W),) * FLOW,
        in_specs=[SM] + [VM] * len(arrays),
        out_specs=(AN,) * FLOW,
        scratch_shapes=[
            pltpu.VMEM((4, SPAN + 2, 3, C, W), bf16),
            pltpu.VMEM((2, SPAN, C, W), f32),
            pltpu.VMEM((2, BAND, C, W), f32),
            pltpu.VMEM((FLOW, CHUNK, C, W), bf16),
            pltpu.SemaphoreType.DMA((FLOW,)),
        ],
        compiler_params=GRANT,
        name="relax",
    )(info, *arrays)


def opened(info, *arrays):
    return pl.pallas_call(
        opening_kernel,
        out_shape=shape(BAND, C, W, dtype=f32),
        in_specs=[SM] + [VM] * len(arrays),
        out_specs=VM,
        scratch_shapes=[
            pltpu.VMEM((2, SPAN + 2, 3, C, W), bf16),
            pltpu.VMEM((1, SPAN, C, W), f32),
        ],
        compiler_params=GRANT,
        name="opening",
    )(info, *arrays)


def rims(half, b, *arrays):
    total = HALO - LEAD if half else LEAD + BAND
    return pl.pallas_call(
        functools.partial(rim_kernel, half),
        out_shape=(shape(total, C, W),) * 2,
        in_specs=[SM] + [VM] * len(arrays),
        out_specs=(VM, VM),
        scratch_shapes=[pltpu.VMEM((SUB, BAND, C, W), bf16)],
        compiler_params=GRANT,
    )(b, *arrays)


def finish(info, arrays):
    return pl.pallas_call(
        finish_kernel,
        out_shape=shape(2 * IMAGES * C * BAND, W, dtype=f32),
        in_specs=[SM] + [AN] * SUB,
        out_specs=AN,
        scratch_shapes=[
            pltpu.VMEM((IMAGES, 2, BAND, C, W), bf16),
            pltpu.VMEM((IMAGES, 2, BAND * C, W), f32),
            pltpu.VMEM((IMAGES, 2, BAND * C, W), f32),
            pltpu.SemaphoreType.DMA((IMAGES,)),
            pltpu.SemaphoreType.DMA((IMAGES, 2)),
        ],
        compiler_params=GRANT,
        name="finish",
    )(info, *arrays)


def order(sub, chunks):
    return pl.pallas_call(
        order_kernel,
        out_shape=(shape(STEPS, BAND, C, W), shape(STEPS, 3, C, W)),
        in_specs=[SM] + [VM] * SUB,
        out_specs=(VM, VM),
        cost_estimate=pl.CostEstimate(flops=0, bytes_accessed=5_000_000, transcendentals=0),
        compiler_params=GRANT,
        name="order",
    )(sub, *chunks)


def sweep(stage, closing, info, *arrays):
    if closing:
        out_shape = (shape(2, BAND, C, W),) * SUB
        extra = [pltpu.VMEM((SUB, 2, BAND, C, W), bf16), pltpu.SemaphoreType.DMA((SUB,))]
    else:
        out_shape = (shape(BAND, C, W, dtype=f32), shape(BAND, C, W))
        extra = []
    return pl.pallas_call(
        functools.partial(sweep_kernel, stage, closing),
        out_shape=out_shape,
        in_specs=[SM] + [VM] * len(arrays),
        out_specs=(AN,) * SUB if closing else (VM, VM),
        scratch_shapes=[pltpu.VMEM((2, WIN + 2, 3, C, W), bf16), pltpu.VMEM((WIN, C, W), f32)] + extra,
        compiler_params=GRANT,
        name="sweep",
    )(info, *arrays)


def cycle(weights, image, guess):
    layers, rows = lax.axis_size("layer"), lax.axis_size("rows")
    groups = layers // SUB
    l, z = lax.axis_index("layer"), lax.axis_index("rows")
    sub, group = lax.rem(l, SUB), l // SUB
    mine = jnp.where(sub == home(1), 1, jnp.where(sub == home(2), 2, 0))

    lead = jnp.where(group == 0, 1, 0)
    info = jnp.stack([z, lax.rem(sub, FLOW), lead, mine, sub // FLOW, group]).astype(jnp.int32)
    rim_up, rim_dn = edges(info, guess.reshape(-1, W), image.reshape(-1, W))

    small = weights[:M]
    up = lax.ppermute(rim_up, "rows", [(i, i + 1) for i in range(rows - 1)])
    dn = lax.ppermute(rim_dn, "rows", [(i + 1, i) for i in range(rows - 1)])
    following = lax.ppermute(small, "layer", [(i + 1, i) for i in range(layers - 1)])
    opening = small
    for b in range(1, IMAGES):
        got = lax.ppermute(small, "layer", [(0, home(b))])
        opening = jnp.where(l == home(b), got, opening)

    sends = relax(info, guess.reshape(-1, W), up, dn, weights, following)

    def pairs(half, k):
        return [
            (SUB * g + FLOW * half + (b + k) % FLOW, SUB * g + home(b))
            for g in range(groups)
            for b in range(IMAGES)
        ]

    received = [
        [lax.ppermute(sends[k], "layer", pairs(h, k)) for k in range(FLOW)] for h in range(HALVES)
    ]

    v1 = opened(info, image.reshape(-1, W), up, dn, opening)

    def among_sweepers(value, ahead, by, live):
        pairs = []
        for g in live:
            for b in range(IMAGES):
                for k in range(rows):
                    if 0 <= k + by < rows:
                        source = (SUB * g + home(b)) * rows + k
                        target = (SUB * (g + ahead) + home(b)) * rows + k + by
                        pairs.append((source, target))
        return lax.ppermute(value, ("layer", "rows"), pairs)

    images = mine.astype(jnp.int32).reshape(1)
    up, dn = rims(0, images, *received[0], v1)
    up0, dn0 = among_sweepers(up, 0, 1, range(groups)), among_sweepers(dn, 0, -1, range(groups))
    up, dn = rims(1, images, *received[1])
    up1, dn1 = among_sweepers(up, 0, 1, range(groups)), among_sweepers(dn, 0, -1, range(groups))
    d, w = order(images, received[0] + received[1])

    handed = []
    for stage in range(groups - 1):
        state, edge = sweep(stage, False, info, v1, d, up0, dn0, up1, dn1, w, *handed[-3:])
        for value, by in ((state, 0), (edge, 1), (edge, -1)):
            handed.append(among_sweepers(value, 1, by, [stage]))
    results = sweep(groups - 1, True, info, v1, d, up0, dn0, up1, dn1, w, *handed)

    back = []
    for h in range(HALVES):
        for k in range(FLOW):
            back.append(lax.ppermute(results[FLOW * h + k], "layer", [(t, s) for s, t in pairs(h, k)]))
    return finish(info, back).reshape(guess.shape)


def solution(mesh):
    return jax.shard_map(
        cycle,
        mesh=mesh,
        in_specs=(
            P("layer", None, None),
            P(None, None, "rows", None),
            P("layer", None, None, "rows", None),
        ),
        out_specs=P("layer", None, None, "rows", None),
        check_vma=False,
    )
```
